32 devices in a mesh: fsdp: 2 (over core), ctx: 4 (over y, x), tp: 4 (over z).
Axes of the slice: x: 2, y: 2, z: 4, core: 2. Of those that a mesh axis runs over, the one named last changes fastest.
Arguments:
- tokens: bfloat16 [4096, 1024], P(('fsdp', 'ctx')), may hold values from -6 to 6
- cotangent: bfloat16 [4096, 1024], P(('fsdp', 'ctx')), may hold values from -6 to 6
- lengths: int32 [2, 3], P('fsdp'), may hold values from 1 to 1365, 2048 in all within a row
- attn_gain: bfloat16 [1024], P(('fsdp', 'ctx')), may hold values from 0.099609375 to 1.8984375
- query_proj: bfloat16 [1024, 512], P(('fsdp', 'ctx'), 'tp'), may hold values from -0.1875 to 0.1875
- key_proj: bfloat16 [1024, 512], P(('fsdp', 'ctx'), 'tp'), may hold values from -0.1875 to 0.1875
- value_proj: bfloat16 [1024, 1024], P(('fsdp', 'ctx'), 'tp'), may hold values from -0.1875 to 0.1875
- gate_proj: bfloat16 [1024, 1024], P(('fsdp', 'ctx'), 'tp'), may hold values from -0.1875 to 0.1875
- rank_down: bfloat16 [1024, 16], P(('fsdp', 'ctx')), may hold values from -0.1875 to 0.1875
- rank_up: bfloat16 [16, 512], P(None, 'tp'), may hold values from -1.5 to 1.5
- rank_bias: bfloat16 [512], P('tp'), may hold values from -1 to 8
- head_gain: bfloat16 [256], replicated, may hold values from 0.099609375 to 1.8984375
- output_proj: bfloat16 [1024, 1024], P('tp', ('fsdp', 'ctx')), may hold values from -0.375 to 0.375
- ffn_gain: bfloat16 [1024], P(('fsdp', 'ctx')), may hold values from 0.099609375 to 1.8984375
- ffn_gate: bfloat16 [1024, 2816], P(('fsdp', 'ctx'), 'tp'), may hold values from -0.1875 to 0.1875
- ffn_up: bfloat16 [1024, 2816], P(('fsdp', 'ctx'), 'tp'), may hold values from -0.1875 to 0.1875
- ffn_down: bfloat16 [2816, 1024], P('tp', ('fsdp', 'ctx')), may hold values from -0.109375 to 0.109375
Outputs:
- block_out: bfloat16 [4096, 1024], P(('fsdp', 'ctx'))
- tokens_grad: float32 [4096, 1024], P(('fsdp', 'ctx'))
- attn_gain_grad: float32 [1024], P(('fsdp', 'ctx'))
- query_grad: float32 [1024, 512], P(('fsdp', 'ctx'), 'tp')
- key_grad: float32 [1024, 512], P(('fsdp', 'ctx'), 'tp')
- value_grad: float32 [1024, 1024], P(('fsdp', 'ctx'), 'tp')
- gate_grad: float32 [1024, 1024], P(('fsdp', 'ctx'), 'tp')
- rank_down_grad: float32 [1024, 16], P(('fsdp', 'ctx'))
- rank_up_grad: float32 [16, 512], P(None, 'tp')
- rank_bias_grad: float32 [512], P('tp')
- head_gain_grad: float32 [256], replicated
- output_grad: float32 [1024, 1024], P('tp', ('fsdp', 'ctx'))
- ffn_gain_grad: float32 [1024], P(('fsdp', 'ctx'))
- ffn_gate_grad: float32 [1024, 2816], P(('fsdp', 'ctx'), 'tp')
- ffn_up_grad: float32 [1024, 2816], P(('fsdp', 'ctx'), 'tp')
- ffn_down_grad: float32 [2816, 1024], P('tp', ('fsdp', 'ctx'))
The draws below stay inside these ranges and needn't reach their ends.
Inputs may be any that keep to these rules, and one draw needn't show every extreme that they name: Row g holds the lengths of the 3 sequences of group g in order; each row sums to 2048, and its largest entry is exactly 1365.
All inputs are finite; a program needn't handle non-finite values.
Results may differ from the reference program's by a relative error of at most 0.025.
Values may be sent and summed in bfloat16 or wider, within the bound.
No kernel may reach another device: no remote copies, remote signals or barrier semaphores. Data moves between devices by JAX's collectives and lax.ppermute only.
A program may use at most 128 MiB of HBM per device.

```python
import math
import jax
import jax.numpy as jnp
import numpy as np
from jax import lax

D = 1024
HEADS = 4
HEAD_K = 128
HEAD_V = 256
FF = 2816
RANK = 16
SPAN = 64
TOK_DEV = 512
SEQS = 3
TOKENS = 4096
N_FSDP = 2
N_CTX = 4


def block_levels(own_key, extent, split, least, top_value):
    loudness = 1.0
    for position, blocks in split:
        heights = jax.random.uniform(jax.random.fold_in(jax.random.fold_in(own_key, 6), position), (blocks,), jnp.float32, least / len(split), top_value / len(split))
        loudness = loudness * jnp.repeat(jnp.exp(heights), extent[position] // blocks).reshape((-1,) + (1,) * (len(extent) - 1 - position))
    return loudness


def profile(number_of, total, bound, slope):
    portions = [(1 << 20) // math.isqrt(grade ** slope) + 1 for grade in range(2, number_of + 1)]
    surplus, counts = total - bound - (number_of - 1), [1] * (number_of - 1)
    while surplus > 0:
        free = [i for i in range(number_of - 1) if counts[i] < bound]
        whole, budget = sum([portions[i] for i in free]), surplus
        for i in free:
            more = min(bound - counts[i], max(1, budget * portions[i] // whole), surplus)
            counts[i] = counts[i] + more
            surplus = surplus - more
    return np.array([bound] + counts)


def uneven(rng, amount, total, most, lean):
    if amount == 2:
        one = jax.random.randint(rng, (), max(1, total - most), min(most, total - 1) + 1)
        return jnp.stack([one, total - one])
    tallies = jnp.asarray(profile(amount, total, most, lean), jnp.int32)
    twos = (amount - 1) // 2
    giver, receiver = tallies[1:1 + 2 * twos:2], tallies[2:2 + 2 * twos:2]
    margin = jnp.minimum(giver - 1, most - receiver)
    passed = jax.random.randint(jax.random.fold_in(rng, 1), (twos,), 0, 1 << 20) % (margin + 1)
    tallies = tallies.at[1:1 + 2 * twos:2].set(giver - passed).at[2:2 + 2 * twos:2].set(receiver + passed)
    return tallies[jax.random.permutation(jax.random.fold_in(rng, 2), amount)]


def normal_values(stream_key, dims, deviation, limit, shards=(), held_as=jnp.bfloat16):
    drawn = deviation * jax.random.normal(stream_key, dims, jnp.float32)
    if shards:
        drawn = drawn * block_levels(stream_key, dims, shards, -0.22, 0.18)
    return jnp.clip(drawn, -limit, limit).astype(held_as)


def setup_inputs(seed: int = 0) -> dict:
    arg_keys = jax.random.split(jax.random.key(seed), 18)
    tokens = normal_values(arg_keys[0], (TOKENS, D), 1.0, 6.0, ((0, 8),))
    cotangent = normal_values(arg_keys[1], (TOKENS, D), 1.0, 6.0, ((0, 8),))
    lengths = jax.vmap(lambda own: uneven(own, SEQS, TOK_DEV * N_CTX, 2 * TOK_DEV * N_CTX // 3, 0))(jax.random.split(arg_keys[2], N_FSDP)).reshape((N_FSDP, SEQS)).astype(jnp.int32)
    attn_gain = jnp.clip(1.0 + 0.18 * jax.random.normal(arg_keys[3], (D,), jnp.float32), 0.099609375, 1.8984375).astype(jnp.bfloat16)
    query_proj = normal_values(arg_keys[4], (D, HEADS * HEAD_K), D ** -0.5, 0.1875, ((0, 8), (1, 4)))
    key_proj = normal_values(arg_keys[5], (D, HEADS * HEAD_K), D ** -0.5, 0.1875, ((0, 8), (1, 4)))
    value_proj = normal_values(arg_keys[6], (D, HEADS * HEAD_V), D ** -0.5, 0.1875, ((0, 8), (1, 4)))
    gate_proj = normal_values(arg_keys[7], (D, HEADS * HEAD_V), D ** -0.5, 0.1875, ((0, 8), (1, 4)))
    rank_down = normal_values(arg_keys[8], (D, RANK), D ** -0.5, 0.1875, ((0, 8),))
    rank_up = normal_values(arg_keys[9], (RANK, HEADS * HEAD_K), RANK ** -0.5, 1.5, ((1, 4),))
    rank_bias = jnp.clip(-1.0 + 9.0 * jax.random.uniform(arg_keys[10], (HEADS * HEAD_K,), jnp.float32) ** block_levels(arg_keys[10], (HEADS * HEAD_K,), ((0, 4),), -0.2, 0.2), -1.0, 8.0).astype(jnp.bfloat16)
    head_gain = jnp.clip(1.0 + 0.18 * jax.random.normal(arg_keys[11], (HEAD_V,), jnp.float32), 0.099609375, 1.8984375).astype(jnp.bfloat16)
    output_proj = normal_values(arg_keys[12], (HEADS * HEAD_V, D), (HEADS * HEAD_V // 4) ** -0.5, 0.375, ((0, 4), (1, 8)))
    ffn_gain = jnp.clip(1.0 + 0.18 * jax.random.normal(arg_keys[13], (D,), jnp.float32), 0.099609375, 1.8984375).astype(jnp.bfloat16)
    ffn_gate = normal_values(arg_keys[14], (D, FF), D ** -0.5, 0.1875, ((0, 8), (1, 4)))
    ffn_up = normal_values(arg_keys[15], (D, FF), D ** -0.5, 0.1875, ((0, 8), (1, 4)))
    ffn_down = normal_values(arg_keys[16], (FF, D), FF ** -0.5, 0.109375, ((0, 4), (1, 8)))
    return {"tokens": tokens, "cotangent": cotangent, "lengths": lengths, "attn_gain": attn_gain, "query_proj": query_proj, "key_proj": key_proj, "value_proj": value_proj, "gate_proj": gate_proj, "rank_down": rank_down, "rank_up": rank_up, "rank_bias": rank_bias, "head_gain": head_gain, "output_proj": output_proj, "ffn_gain": ffn_gain, "ffn_gate": ffn_gate, "ffn_up": ffn_up, "ffn_down": ffn_down}


exact_mode = lax.Precision.HIGHEST
epsilon = 1e-06
logit_scale = 16.0

def rms_scale(field_in):
    return lax.rsqrt(lax.optimization_barrier(jnp.mean(field_in * field_in, axis=-1, keepdims=True)) + epsilon)

def to_heads(matrix, width):
    return matrix.reshape(matrix.shape[0], -1, width).transpose(1, 0, 2)

def from_heads(tensor):
    return tensor.transpose(1, 0, 2).reshape(tensor.shape[1], -1)

def to_blocks(array_in, block_rows):
    return array_in.reshape(array_in.shape[0], -1, block_rows, array_in.shape[2]).transpose(1, 0, 2, 3)

def from_blocks(array_in):
    return array_in.transpose(1, 0, 2, 3).reshape(array_in.shape[1], -1, array_in.shape[3])

def segment_ids(length_row, positions):
    seq_ends = jnp.cumsum(length_row)
    return lax.optimization_barrier(jnp.sum(jnp.where(positions[:, None] >= seq_ends[None, :], 1, 0), axis=1)).astype(jnp.int32)

def first_rows(length_row, positions):
    seq_starts = jnp.cumsum(length_row) - length_row
    return jnp.any(positions[:, None] == seq_starts[None, :], axis=1)

def span_preceding(segment, before, block_rows):
    segments = segment.reshape(-1, block_rows)
    return jnp.concatenate([jnp.reshape(before, (1,)).astype(jnp.int32), segments[:-1, -1].astype(jnp.int32)])

def span_terms(scaled, key_rows, cumulative, segment):
    places = jnp.arange(segment.shape[0])
    visible = (segment[:, None] == segment[None, :]) & (places[:, None] >= places[None, :])
    query_decayed = scaled * jnp.exp(cumulative)
    key_decayed = key_rows * jnp.exp(-cumulative)
    raw_scores = jnp.einsum('hic,hjc->hij', query_decayed, key_decayed, precision=exact_mode)
    scores = jnp.where(visible[None, :, :], raw_scores, 0.0)
    return (visible, query_decayed, key_decayed, scores)

def span_forward(carry_state, pieces):
    scaled, key_rows, value_rows, cumulative, segment, before = pieces
    visible, query_decayed, key_decayed, scores = span_terms(scaled, key_rows, cumulative, segment)
    carried = segment == before
    entering = jnp.where(carried[None, :, None], query_decayed, 0.0)
    output = jnp.einsum('hij,hjv->hiv', scores, value_rows, precision=exact_mode) + jnp.einsum('hic,hcv->hiv', entering, carry_state, precision=exact_mode)
    ending = cumulative[:, -1, :]
    tail_decay = jnp.where((segment == segment[-1])[None, :, None], jnp.exp(ending[:, None, :] - cumulative), 0.0)
    fresh_state = jnp.einsum('hjc,hjv->hcv', key_rows * tail_decay, value_rows, precision=exact_mode)
    kept_decay = jnp.where(carried[-1], jnp.exp(ending), 0.0)
    return (kept_decay[:, :, None] * carry_state + fresh_state, (output, carry_state))

def span_backward(grad_after, pieces):
    scaled, key_rows, value_rows, cumulative, segment, before, carry_state, out_grad = pieces
    visible, query_decayed, key_decayed, scores = span_terms(scaled, key_rows, cumulative, segment)
    carried = segment == before
    lifted = jnp.where(carried[None, :, None], jnp.exp(cumulative), 0.0)
    entering = jnp.where(carried[None, :, None], query_decayed, 0.0)
    ending = cumulative[:, -1, :]
    tail_decay = jnp.where((segment == segment[-1])[None, :, None], jnp.exp(ending[:, None, :] - cumulative), 0.0)
    dscore = jnp.where(visible[None, :, :], jnp.einsum('hiv,hjv->hij', out_grad, value_rows, precision=exact_mode), 0.0)
    dscaled = jnp.exp(cumulative) * jnp.einsum('hij,hjc->hic', dscore, key_decayed, precision=exact_mode) + lifted * jnp.einsum('hiv,hcv->hic', out_grad, carry_state, precision=exact_mode)
    key_grad = jnp.exp(-cumulative) * jnp.einsum('hij,hic->hjc', dscore, query_decayed, precision=exact_mode) + tail_decay * jnp.einsum('hjv,hcv->hjc', value_rows, grad_after, precision=exact_mode)
    dvalues = jnp.einsum('hij,hiv->hjv', scores, out_grad, precision=exact_mode) + jnp.einsum('hjc,hcv->hjv', key_rows * tail_decay, grad_after, precision=exact_mode)
    kept_decay = jnp.where(carried[-1], jnp.exp(ending), 0.0)
    grad_before = jnp.einsum('hic,hiv->hcv', entering, out_grad, precision=exact_mode) + kept_decay[:, :, None] * grad_after
    return (grad_before, (dscaled, key_grad, dvalues))

def mixer_forward(scaled, key_rows, value_rows, log_decay, segment, preceding, block_rows):
    head_count, row_count, key_width = scaled.shape
    cumulative = jnp.cumsum(to_blocks(log_decay, block_rows), axis=2)
    segments = segment.reshape(row_count // block_rows, block_rows)
    initial = jnp.zeros((head_count, key_width, value_rows.shape[2]), jnp.float32)
    pieces = (to_blocks(scaled, block_rows), to_blocks(key_rows, block_rows), to_blocks(value_rows, block_rows), cumulative, segments, preceding)
    last_state, (outputs, states) = lax.scan(span_forward, initial, pieces)
    return (from_blocks(outputs), last_state, states, cumulative)

def mixer_backward(scaled, key_rows, value_rows, cumulative, segment, preceding, states, out_grad, block_rows):
    head_count, row_count, key_width = scaled.shape
    segments = segment.reshape(row_count // block_rows, block_rows)
    initial = jnp.zeros((head_count, key_width, value_rows.shape[2]), jnp.float32)
    pieces = (to_blocks(scaled, block_rows), to_blocks(key_rows, block_rows), to_blocks(value_rows, block_rows), cumulative, segments, preceding, states, to_blocks(out_grad, block_rows))
    first_grad, (dscaled, key_grad, dvalues) = lax.scan(span_backward, initial, pieces, reverse=True)
    return (first_grad, from_blocks(dscaled), from_blocks(key_grad), from_blocks(dvalues))

def suffix_within(term, segment, seq_count):
    reverse_total = jnp.cumsum(term[:, ::-1, :], axis=1)[:, ::-1, :]
    labels = jnp.arange(seq_count)
    member = jnp.where(segment[:, None] == labels[None, :], 1.0, 0.0)
    seg_sums = jnp.einsum('rs,hrk->hsk', member, term, precision=exact_mode)
    later_mask = jnp.where(segment[:, None] < labels[None, :], 1.0, 0.0)
    return reverse_total - jnp.einsum('rs,hsk->hrk', later_mask, seg_sums, precision=exact_mode)

def group_pass(tokens, cotangent, length_row, weights):
    attn_gain, query_proj, key_proj, value_proj, gate_proj, rank_down, rank_up, rank_bias, head_gain, output_proj, ffn_gain, ffn_gate, ffn_up, ffn_down = weights
    row_count = tokens.shape[0]
    positions = jnp.arange(row_count)
    segment = segment_ids(length_row, positions)
    opening = first_rows(length_row, positions)
    preceding = span_preceding(segment, jnp.int32(-1), SPAN)
    inputs = tokens.astype(jnp.float32)
    scale_one = rms_scale(inputs)
    gain_one = attn_gain.astype(jnp.float32)
    normed = (inputs * scale_one * gain_one).astype(jnp.bfloat16)
    query_rows = jnp.dot(normed, query_proj, preferred_element_type=jnp.float32).astype(jnp.bfloat16)
    key_rows = jnp.dot(normed, key_proj, preferred_element_type=jnp.float32).astype(jnp.bfloat16)
    value_rows = jnp.dot(normed, value_proj, preferred_element_type=jnp.float32).astype(jnp.bfloat16)
    gate_pre = jnp.dot(normed, gate_proj, preferred_element_type=jnp.float32)
    low_rank = jnp.dot(normed, rank_down, preferred_element_type=jnp.float32).astype(jnp.bfloat16)
    forget_pre = jnp.dot(low_rank, rank_up, preferred_element_type=jnp.float32) + rank_bias.astype(jnp.float32)
    log_decay = jax.nn.log_sigmoid(forget_pre) / logit_scale
    scaled = to_heads(query_rows.astype(jnp.float32), HEAD_K) * HEAD_K ** (-0.5)
    key_heads = to_heads(key_rows.astype(jnp.float32), HEAD_K)
    value_heads = to_heads(value_rows.astype(jnp.float32), HEAD_V)
    decay_heads = to_heads(log_decay, HEAD_K)
    mixed_heads, last_state, states, cumulative = mixer_forward(scaled, key_heads, value_heads, decay_heads, segment, preceding, SPAN)
    head_scale = rms_scale(mixed_heads)
    unit_heads = mixed_heads * head_scale
    gain_head = head_gain.astype(jnp.float32)
    gate_sig = jax.nn.sigmoid(gate_pre)
    swish_gate = gate_pre * gate_sig
    gated_unit = from_heads(unit_heads * gain_head)
    attended = (gated_unit * swish_gate).astype(jnp.bfloat16)
    hidden_in = inputs + jnp.dot(attended, output_proj, preferred_element_type=jnp.float32)
    scale_two = rms_scale(hidden_in)
    gain_two = ffn_gain.astype(jnp.float32)
    normed_two = (hidden_in * scale_two * gain_two).astype(jnp.bfloat16)
    gate_val = jnp.dot(normed_two, ffn_gate, preferred_element_type=jnp.float32)
    up_val = jnp.dot(normed_two, ffn_up, preferred_element_type=jnp.float32)
    gate_act = jax.nn.sigmoid(gate_val)
    hidden = (gate_val * gate_act * up_val).astype(jnp.bfloat16)
    block_out = (hidden_in + jnp.dot(hidden, ffn_down, preferred_element_type=jnp.float32)).astype(jnp.bfloat16)
    out_grad = cotangent.astype(jnp.float32)
    down_grad = jnp.dot(hidden.T, cotangent, preferred_element_type=jnp.float32)
    hidden_grad = jnp.dot(cotangent, ffn_down.T, preferred_element_type=jnp.float32)
    gate_back = (hidden_grad * up_val * gate_act * (1.0 + gate_val * (1.0 - gate_act))).astype(jnp.bfloat16)
    up_back = (hidden_grad * gate_val * gate_act).astype(jnp.bfloat16)
    ffn_gate_grad = jnp.dot(normed_two.T, gate_back, preferred_element_type=jnp.float32)
    ffn_up_grad = jnp.dot(normed_two.T, up_back, preferred_element_type=jnp.float32)
    normed_two_grad = jnp.dot(gate_back, ffn_gate.T, preferred_element_type=jnp.float32) + jnp.dot(up_back, ffn_up.T, preferred_element_type=jnp.float32)
    ffn_gain_grad = lax.optimization_barrier(jnp.sum(normed_two_grad * hidden_in * scale_two, axis=0))
    weighted_two = normed_two_grad * gain_two
    hidden_in_grad = out_grad + scale_two * weighted_two - hidden_in * scale_two ** 3 * lax.optimization_barrier(jnp.mean(weighted_two * hidden_in, axis=-1, keepdims=True))
    residual_back = hidden_in_grad.astype(jnp.bfloat16)
    output_grad = jnp.dot(attended.T, residual_back, preferred_element_type=jnp.float32)
    attended_grad = jnp.dot(residual_back, output_proj.T, preferred_element_type=jnp.float32)
    unit_gain_grad = to_heads(attended_grad * swish_gate, HEAD_V)
    head_gain_grad = lax.optimization_barrier(jnp.sum(unit_gain_grad * unit_heads, axis=(0, 1)))
    gate_pre_back = (attended_grad * gated_unit * gate_sig * (1.0 + gate_pre * (1.0 - gate_sig))).astype(jnp.bfloat16)
    unit_grad = unit_gain_grad * gain_head
    mixed_grad = head_scale * (unit_grad - unit_heads * lax.optimization_barrier(jnp.mean(unit_grad * unit_heads, axis=-1, keepdims=True)))
    first_grad, dscaled, key_grad_heads, value_grad_heads = mixer_backward(scaled, key_heads, value_heads, cumulative, segment, preceding, states, mixed_grad, SPAN)
    decay_term = scaled * dscaled - key_heads * key_grad_heads
    decay_grad = jnp.where(opening[None, :, None], 0.0, suffix_within(decay_term, segment, SEQS))
    forget_grad = from_heads(decay_grad) * jax.nn.sigmoid(-forget_pre) / logit_scale
    bias_grad = lax.optimization_barrier(jnp.sum(forget_grad, axis=0))
    forget_back = forget_grad.astype(jnp.bfloat16)
    rank_up_grad = jnp.dot(low_rank.T, forget_back, preferred_element_type=jnp.float32)
    rank_back = jnp.dot(forget_back, rank_up.T, preferred_element_type=jnp.float32).astype(jnp.bfloat16)
    query_back = from_heads(dscaled * HEAD_K ** (-0.5)).astype(jnp.bfloat16)
    key_back = from_heads(key_grad_heads).astype(jnp.bfloat16)
    value_back = from_heads(value_grad_heads).astype(jnp.bfloat16)
    rank_down_grad = jnp.dot(normed.T, rank_back, preferred_element_type=jnp.float32)
    query_grad = jnp.dot(normed.T, query_back, preferred_element_type=jnp.float32)
    key_grad = jnp.dot(normed.T, key_back, preferred_element_type=jnp.float32)
    value_grad = jnp.dot(normed.T, value_back, preferred_element_type=jnp.float32)
    gate_grad = jnp.dot(normed.T, gate_pre_back, preferred_element_type=jnp.float32)
    normed_grad = jnp.dot(query_back, query_proj.T, preferred_element_type=jnp.float32)
    normed_grad = normed_grad + jnp.dot(key_back, key_proj.T, preferred_element_type=jnp.float32)
    normed_grad = normed_grad + jnp.dot(value_back, value_proj.T, preferred_element_type=jnp.float32)
    normed_grad = normed_grad + jnp.dot(gate_pre_back, gate_proj.T, preferred_element_type=jnp.float32)
    normed_grad = normed_grad + jnp.dot(rank_back, rank_down.T, preferred_element_type=jnp.float32)
    attn_gain_grad = lax.optimization_barrier(jnp.sum(normed_grad * inputs * scale_one, axis=0))
    weighted_one = normed_grad * gain_one
    tokens_grad = hidden_in_grad + scale_one * weighted_one - inputs * scale_one ** 3 * lax.optimization_barrier(jnp.mean(weighted_one * inputs, axis=-1, keepdims=True))
    grad_parts = (attn_gain_grad, query_grad, key_grad, value_grad, gate_grad, rank_down_grad, rank_up_grad, bias_grad, head_gain_grad, output_grad, ffn_gain_grad, ffn_gate_grad, ffn_up_grad, down_grad)
    return (block_out, tokens_grad, grad_parts)

def reference(tokens, cotangent, lengths, attn_gain, query_proj, key_proj, value_proj, gate_proj, rank_down, rank_up, rank_bias, head_gain, output_proj, ffn_gain, ffn_gate, ffn_up, ffn_down):
    group_size = TOK_DEV * N_CTX
    weights = (attn_gain, query_proj, key_proj, value_proj, gate_proj, rank_down, rank_up, rank_bias, head_gain, output_proj, ffn_gain, ffn_gate, ffn_up, ffn_down)

    def visit_group(totals, pieces):
        group_rows, cot_rows, length_row = pieces
        out_rows, grad_rows, grad_parts = group_pass(group_rows, cot_rows, length_row, weights)
        return (jax.tree.map(lambda total, part: total + part, totals, grad_parts), (out_rows, grad_rows))
    initial = tuple((jnp.zeros(weight.shape, jnp.float32) for weight in weights))
    totals, (out_rows, grad_rows) = lax.scan(visit_group, initial, (tokens.reshape(N_FSDP, group_size, D), cotangent.reshape(N_FSDP, group_size, D), lengths))
    block_out = out_rows.reshape(TOKENS, D)
    tokens_grad = grad_rows.reshape(TOKENS, D)
    return (block_out, tokens_grad, totals[0], totals[1], totals[2], totals[3], totals[4], totals[5], totals[6], totals[7], totals[8], totals[9], totals[10], totals[11], totals[12], totals[13])
```

```python
import functools

import jax
import jax.numpy as jnp
from jax import lax
from jax.experimental import pallas as pl
from jax.experimental.pallas import tpu as pltpu
from jax.sharding import PartitionSpec as P

HEAD_K = 128
HEAD_V = 256
SPAN = 64
PAIR = 128
LANES = 128
epsilon = 1e-06
logit_scale = 16.0
bf16 = jnp.bfloat16
f32 = jnp.float32


def target(count, index, hop):
    return index ^ hop if count & (count - 1) == 0 else (index + hop) % count


def origin(count, index, hop):
    return index ^ hop if count & (count - 1) == 0 else (index - hop + count) % count


def swap(value, axis, hop):
    count = lax.axis_size(axis)
    return lax.ppermute(value, axis, [(i, target(count, i, hop)) for i in range(count)])


def pick(value, position, size, dim):
    return lax.dynamic_slice_in_dim(value, position * size, size, dim)


def spread(value, axis, dim):
    count, mine = lax.axis_size(axis), lax.axis_index(axis)
    size = value.shape[dim]
    shape = value.shape[:dim] + (count * size,) + value.shape[dim + 1 :]
    pieces = [value] + [swap(value, axis, hop) for hop in range(1, count)]
    full = jnp.zeros(shape, value.dtype)
    for hop, piece in enumerate(pieces):
        full = lax.dynamic_update_slice_in_dim(
            full, piece, origin(count, mine, hop) * size, dim
        )
    return full


def spread_two(value, outer, inner, dim):
    outer_count, outer_mine = lax.axis_size(outer), lax.axis_index(outer)
    inner_count, inner_mine = lax.axis_size(inner), lax.axis_index(inner)
    size = value.shape[dim]
    shape = (
        value.shape[:dim] + (outer_count * inner_count * size,) + value.shape[dim + 1 :]
    )
    near = [value] + [swap(value, inner, hop) for hop in range(1, inner_count)]
    full = jnp.zeros(shape, value.dtype)
    for hop, piece in enumerate(near):
        column = origin(inner_count, inner_mine, hop)
        for step in range(outer_count):
            row = origin(outer_count, outer_mine, step)
            part = piece if step == 0 else swap(piece, outer, step)
            full = lax.dynamic_update_slice_in_dim(
                full, part, (row * inner_count + column) * size, dim
            )
    return full


def collect(value, axis, dim):
    count, mine = lax.axis_size(axis), lax.axis_index(axis)
    size = value.shape[dim] // count
    total = pick(value, mine, size, dim).astype(f32)
    for hop in range(1, count):
        piece = pick(value, target(count, mine, hop), size, dim)
        total = total + swap(piece, axis, hop).astype(f32)
    return total


def collect_two(value, outer, inner, dim):
    return collect(collect(value, outer, dim).astype(bf16), inner, dim)


def whole_sum(value, axis):
    total = value
    for hop in range(1, lax.axis_size(axis)):
        total = total + swap(value, axis, hop)
    return total


def chained(packed, axis, backward):
    count = lax.axis_size(axis)
    value = None
    for hop in range(count - 1, 0, -1):
        pairs = [(i, i + hop) for i in range(count - hop)]
        if backward:
            pairs = [(b, a) for a, b in pairs]
        piece = lax.ppermute(packed, axis, pairs).astype(f32)
        state, decay = piece[:, :HEAD_V], piece[:, HEAD_V : HEAD_V + 1]
        value = state if value is None else state + decay * value
    return jnp.zeros_like(packed[:, :HEAD_V], f32) if value is None else value


NT = (((1,), (1,)), ((), ()))
NN = (((1,), (0,)), ((), ()))
TN = (((0,), (0,)), ((), ()))


def mm(left, right, dims):
    return lax.dot_general(
        left.astype(bf16), right.astype(bf16), dims, preferred_element_type=f32
    )


def pair_places():
    rows = lax.broadcasted_iota(jnp.int32, (PAIR, PAIR), 0)
    cols = lax.broadcasted_iota(jnp.int32, (PAIR, PAIR), 1)
    return rows, cols, (rows // SPAN) == (cols // SPAN)


def split_mm(ones, value):
    high = value.astype(bf16)
    rest = value - high.astype(f32)
    middle = rest.astype(bf16)
    low = (rest - middle.astype(f32)).astype(bf16)
    return mm(ones, high, NN) + mm(ones, middle, NN) + mm(ones, low, NN)


SEG, ENTER, TAIL, KEPT, OPEN, DEV_IN, DEV_OUT = range(7)


def decay_kernel(heads, low_at, proj_ref, up_ref, bias_ref, facts_ref, fpre_ref, cum_ref, run_ref, state_ref, pack_ref):
    row_count = proj_ref.shape[0]
    spans = row_count // SPAN
    rows, cols, same = pair_places()
    lower = jnp.where(same & (rows >= cols), 1.0, 0.0).astype(bf16)
    low = proj_ref[:, low_at : low_at + LANES]
    fpre = mm(low, up_ref[...], NN) + bias_ref[...]
    fpre_ref[...] = fpre
    log_decay = (jnp.minimum(fpre, 0.0) - jnp.log1p(jnp.exp(-jnp.abs(fpre)))) * (
        1.0 / logit_scale
    )
    for base in range(0, row_count, PAIR):
        cum_ref[base : base + PAIR, :] = split_mm(lower, log_decay[base : base + PAIR, :])
    for head in range(heads):
        at = slice(head * HEAD_K, (head + 1) * HEAD_K)
        vat = slice(heads * HEAD_K + head * HEAD_V, heads * HEAD_K + (head + 1) * HEAD_V)
        state = jnp.zeros((HEAD_V, HEAD_K), f32)
        offset = jnp.zeros((1, HEAD_K), f32)
        for span in range(spans):
            here = slice(span * SPAN, (span + 1) * SPAN)
            cum = cum_ref[here, at]
            ending = cum[SPAN - 1 : SPAN, :]
            run_ref[here, at] = cum + offset
            offset = offset + ending
            tail = jnp.exp(ending - cum) * facts_ref[here, TAIL : TAIL + 1]
            fresh = mm(proj_ref[here, vat], proj_ref[here, at].astype(f32) * tail, TN)
            kept = jnp.exp(ending) * facts_ref[span * SPAN : span * SPAN + 1, KEPT : KEPT + 1]
            state_ref[head, span] = state
            state = kept * state + fresh
        state_ref[head, spans] = state
        pack_ref[head, :HEAD_V, :] = state.astype(bf16)
        through = jnp.exp(offset) * facts_ref[
            row_count - 1 : row_count, DEV_IN : DEV_IN + 1
        ]
        pack_ref[head, HEAD_V:, :] = jnp.broadcast_to(
            through, (pack_ref.shape[1] - HEAD_V, HEAD_K)
        ).astype(bf16)


def forward_kernel(heads, proj_ref, qg_ref, cum_ref, facts_ref, segrow_ref, local_ref, incoming_ref, gain_ref, att_ref, mixed_ref, state_ref):
    row_count = proj_ref.shape[0]
    spans = row_count // SPAN
    rows, cols, same = pair_places()
    ordered = same & (rows >= cols)
    for head in range(heads):
        at = slice(head * HEAD_K, (head + 1) * HEAD_K)
        vat = slice(heads * HEAD_K + head * HEAD_V, heads * HEAD_K + (head + 1) * HEAD_V)
        incoming = incoming_ref[head]
        product = jnp.ones((1, HEAD_K), f32)
        for span in range(spans):
            state_ref[head, span] = (local_ref[head, span] + product * incoming).astype(bf16)
            ending = cum_ref[span * SPAN + SPAN - 1 : span * SPAN + SPAN, at]
            product = product * (
                jnp.exp(ending) * facts_ref[span * SPAN : span * SPAN + 1, KEPT : KEPT + 1]
            )
        state_ref[head, spans] = (local_ref[head, spans] + product * incoming).astype(bf16)
        gain = gain_ref[...]
        for base in range(0, row_count, PAIR):
            here = slice(base, base + PAIR)
            cum = cum_ref[here, at]
            query = qg_ref[here, at].astype(bf16).astype(f32) * HEAD_K ** (-0.5)
            key = proj_ref[here, at].astype(f32)
            value = proj_ref[here, vat]
            grow = jnp.exp(cum)
            query_decayed = query * grow
            key_decayed = key * jnp.exp(-cum)
            visible = ordered & (facts_ref[here, SEG : SEG + 1] == segrow_ref[:, here])
            scores = jnp.where(visible, mm(query_decayed, key_decayed, NT), 0.0)
            entering = (query_decayed * facts_ref[here, ENTER : ENTER + 1]).astype(bf16)
            inner = mm(scores, value, NN)
            for half in range(PAIR // SPAN):
                mine = slice(half * SPAN, (half + 1) * SPAN)
                span = base // SPAN + half
                place = slice(base + half * SPAN, base + (half + 1) * SPAN)
                mixed = inner[mine, :] + mm(entering[mine, :], state_ref[head, span], NT)
                out_at = slice(head * HEAD_V, (head + 1) * HEAD_V)
                mixed_ref[place, out_at] = mixed
                scale = lax.rsqrt(jnp.mean(mixed * mixed, axis=1, keepdims=True) + epsilon)
                gate_at = slice(
                    heads * HEAD_K + head * HEAD_V, heads * HEAD_K + (head + 1) * HEAD_V
                )
                gate = qg_ref[place, gate_at]
                att_ref[place, out_at] = (
                    mixed * scale * gain * (gate * jax.nn.sigmoid(gate))
                ).astype(bf16)


def gate_kernel(heads, agrad_ref, qg_ref, mixed_ref, run_ref, facts_ref, gain_ref, mgrad_ref, gback_ref, hgain_ref, pack_ref):
    row_count = agrad_ref.shape[0]
    gain = gain_ref[...]
    total = jnp.zeros((1, HEAD_V), f32)
    for head in range(heads):
        at = slice(head * HEAD_K, (head + 1) * HEAD_K)
        out_at = slice(head * HEAD_V, (head + 1) * HEAD_V)
        gate_at = slice(heads * HEAD_K + head * HEAD_V, heads * HEAD_K + (head + 1) * HEAD_V)
        state = jnp.zeros((HEAD_V, HEAD_K), f32)
        for base in range(0, row_count, PAIR):
            here = slice(base, base + PAIR)
            mixed = mixed_ref[here, out_at]
            scale = lax.rsqrt(jnp.mean(mixed * mixed, axis=1, keepdims=True) + epsilon)
            unit = mixed * scale
            gate = qg_ref[here, gate_at]
            sig = jax.nn.sigmoid(gate)
            agrad = agrad_ref[here, out_at]
            gback_ref[here, out_at] = (
                agrad * (unit * gain) * sig * (1.0 + gate * (1.0 - sig))
            ).astype(bf16)
            ugg = agrad * (gate * sig)
            total = total + jnp.sum(ugg * unit, axis=0, keepdims=True)
            ug = ugg * gain
            mgrad = (scale * (ug - unit * jnp.mean(ug * unit, axis=1, keepdims=True))).astype(
                bf16
            )
            mgrad_ref[here, out_at] = mgrad
            query = qg_ref[here, at].astype(bf16).astype(f32) * HEAD_K ** (-0.5)
            lifted = query * jnp.exp(run_ref[here, at]) * facts_ref[here, DEV_IN : DEV_IN + 1]
            state = state + mm(mgrad, lifted, TN)
        pack_ref[head, :HEAD_V, :] = state.astype(bf16)
        through = jnp.exp(run_ref[row_count - 1 : row_count, at]) * facts_ref[
            row_count - 1 : row_count, DEV_IN : DEV_IN + 1
        ]
        pack_ref[head, HEAD_V:, :] = jnp.broadcast_to(
            through, (pack_ref.shape[1] - HEAD_V, HEAD_K)
        ).astype(bf16)
    hgain_ref[...] = total


def backward_kernel(heads, proj_ref, qg_ref, cum_ref, fpre_ref, facts_ref, segrow_ref, state_ref, mgrad_ref, gback_ref, beyond_ref, up_ref, low_at, kvl_ref, out_qg_ref, bias_ref, rup_ref, after_ref):
    row_count = proj_ref.shape[0]
    spans = row_count // SPAN
    rows, cols, same = pair_places()
    ordered = same & (rows >= cols)
    upper = jnp.where(same & (cols >= rows), 1.0, 0.0)
    rank_total = jnp.zeros((row_count, LANES), f32)
    for head in range(heads):
        at = slice(head * HEAD_K, (head + 1) * HEAD_K)
        vat = slice(heads * HEAD_K + head * HEAD_V, heads * HEAD_K + (head + 1) * HEAD_V)
        out_at = slice(head * HEAD_V, (head + 1) * HEAD_V)
        after = beyond_ref[head]
        for span in reversed(range(spans)):
            here = slice(span * SPAN, (span + 1) * SPAN)
            cum = cum_ref[here, at]
            after_ref[span] = after.astype(bf16)
            query = qg_ref[here, at].astype(bf16).astype(f32) * HEAD_K ** (-0.5)
            entering = query * jnp.exp(cum) * facts_ref[here, ENTER : ENTER + 1]
            kept = jnp.exp(cum[SPAN - 1 : SPAN, :]) * facts_ref[
                span * SPAN : span * SPAN + 1, KEPT : KEPT + 1
            ]
            after = kept * after + mm(mgrad_ref[here, out_at], entering, TN)
        bias = jnp.zeros((1, HEAD_K), f32)
        rup = jnp.zeros((LANES, HEAD_K), f32)
        for base in range(0, row_count, PAIR):
            here = slice(base, base + PAIR)
            cum = cum_ref[here, at]
            query = qg_ref[here, at].astype(bf16).astype(f32) * HEAD_K ** (-0.5)
            key = proj_ref[here, at].astype(f32)
            value = proj_ref[here, vat]
            mgrad = mgrad_ref[here, out_at]
            grow = jnp.exp(cum)
            shrink = jnp.exp(-cum)
            query_decayed = (query * grow).astype(bf16)
            key_decayed = (key * shrink).astype(bf16)
            segment = facts_ref[here, SEG : SEG + 1]
            visible = ordered & (segment == segrow_ref[:, here])
            scores = jnp.where(visible, mm(query_decayed, key_decayed, NT), 0.0).astype(bf16)
            dscore = jnp.where(visible, mm(mgrad, value, NT), 0.0).astype(bf16)
            dquery_in = mm(dscore, key_decayed, NN)
            dkey_in = mm(dscore, query_decayed, TN)
            dvalue_in = mm(scores, mgrad, TN)
            terms, carries = [], []
            for half in range(PAIR // SPAN):
                mine = slice(half * SPAN, (half + 1) * SPAN)
                span = base // SPAN + half
                place = slice(span * SPAN, (span + 1) * SPAN)
                state = state_ref[head, span]
                behind = after_ref[span]
                ending = cum[(half + 1) * SPAN - 1 : (half + 1) * SPAN, :]
                tail = jnp.exp(ending - cum[mine, :]) * facts_ref[place, TAIL : TAIL + 1]
                lifted = grow[mine, :] * facts_ref[place, ENTER : ENTER + 1]
                dquery = grow[mine, :] * dquery_in[mine, :] + lifted * mm(
                    mgrad[mine, :], state, NN
                )
                dkey = shrink[mine, :] * dkey_in[mine, :] + tail * mm(
                    value[mine, :], behind, NN
                )
                dvalue = dvalue_in[mine, :] + mm(key[mine, :] * tail, behind, NT)
                out_qg_ref[place, at] = (dquery * HEAD_K ** (-0.5)).astype(bf16)
                kvl_ref[place, at] = dkey.astype(bf16)
                kvl_ref[place, vat] = dvalue.astype(bf16)
                terms.append(query[mine, :] * dquery - key[mine, :] * dkey)
                carry = jnp.sum(
                    state_ref[head, span + 1].astype(f32) * behind.astype(f32),
                    axis=0,
                    keepdims=True,
                )
                carries.append(facts_ref[place, TAIL : TAIL + 1] * carry)
            later = jnp.where(
                segment == segrow_ref[:, here], upper, 0.0
            ).astype(bf16)
            decay_grad = split_mm(later, jnp.concatenate(terms, axis=0)) + jnp.concatenate(
                carries, axis=0
            )
            decay_grad = jnp.where(facts_ref[here, OPEN : OPEN + 1] > 0.0, 0.0, decay_grad)
            fgrad = decay_grad * jax.nn.sigmoid(-fpre_ref[here, at]) * (1.0 / logit_scale)
            bias = bias + jnp.sum(fgrad, axis=0, keepdims=True)
            fback = fgrad.astype(bf16)
            rup = rup + mm(proj_ref[here, low_at : low_at + LANES], fback, TN)
            rank = mm(fback, up_ref[:, at], NT)
            if head == heads - 1:
                if heads > 1:
                    rank = rank + kvl_ref[here, low_at : low_at + LANES].astype(f32)
                kvl_ref[here, low_at : low_at + LANES] = rank.astype(bf16)
            else:
                if head > 0:
                    rank = rank + kvl_ref[here, low_at : low_at + LANES].astype(f32)
                kvl_ref[here, low_at : low_at + LANES] = rank.astype(bf16)
        bias_ref[:, at] = bias
        rup_ref[:, at] = rup
    out_qg_ref[:, heads * HEAD_K :] = gback_ref[...]


def call(kernel, outs, scratch=()):
    return pl.pallas_call(
        kernel,
        out_shape=outs,
        scratch_shapes=list(scratch),
        compiler_params=pltpu.CompilerParams(vmem_limit_bytes=48 * 1024 * 1024),
    )


def shape_of(*dims, dtype=f32):
    return jax.ShapeDtypeStruct(dims, dtype)


def row_facts(length_row, row_count):
    seq_ends = jnp.cumsum(length_row)
    seq_starts = seq_ends - length_row
    ctx_index = lax.axis_index("ctx")
    first = ctx_index * row_count
    positions = first + jnp.arange(row_count, dtype=jnp.int32)

    def label(places):
        return jnp.sum(
            (places[:, None] >= seq_ends[None, :]).astype(jnp.int32), axis=1
        ).astype(jnp.int32)

    segment = label(positions)
    spans = row_count // SPAN
    span_first = first + jnp.arange(spans, dtype=jnp.int32) * SPAN
    before = jnp.where(span_first > 0, label(span_first - 1), -1)
    last = label(span_first + SPAN - 1)
    opening = jnp.any(positions[:, None] == seq_starts[None, :], axis=1)

    def wide(values):
        return jnp.repeat(values, SPAN)

    columns = (
        segment,
        segment == wide(before),
        segment == wide(last),
        wide(last == before),
        opening,
        segment == before[0],
        segment == last[-1],
        jnp.zeros_like(segment),
    )
    facts = jnp.stack([column.astype(f32) for column in columns], axis=1)
    return facts, segment.astype(f32)[None, :]


def rms_scale(field_in):
    return lax.rsqrt(jnp.mean(field_in * field_in, axis=-1, keepdims=True) + epsilon)


def dot(left, right, dims):
    return lax.dot_general(left, right, dims, preferred_element_type=f32)


def local(
    tokens,
    cotangent,
    lengths,
    attn_gain,
    query_proj,
    key_proj,
    value_proj,
    gate_proj,
    rank_down,
    rank_up,
    rank_bias,
    head_gain,
    output_proj,
    ffn_gain,
    ffn_gate,
    ffn_up,
    ffn_down,
):
    row_count, width = tokens.shape
    tp_count, tp_index = lax.axis_size("tp"), lax.axis_index("tp")
    own_rows = row_count // tp_count
    heads = query_proj.shape[1] // HEAD_K
    key_cols, value_cols = heads * HEAD_K, heads * HEAD_V
    rank = rank_down.shape[1]
    shard = rank_down.shape[0]
    low_at = key_cols + value_cols

    low_block = jnp.concatenate(
        [
            rank_down,
            attn_gain[:, None],
            ffn_gain[:, None],
            jnp.zeros((shard, LANES - rank - 2), bf16),
        ],
        axis=1,
    )
    kvl_w = spread_two(
        jnp.concatenate([key_proj, value_proj, low_block], axis=1), "fsdp", "ctx", 0
    )
    qg_w = spread_two(jnp.concatenate([query_proj, gate_proj], axis=1), "fsdp", "ctx", 0)
    out_w = spread_two(output_proj.T, "fsdp", "ctx", 0)
    ffn_shard = jnp.stack([ffn_gate, ffn_up, ffn_down.T], axis=0)
    kvl_w, ffn_shard = lax.optimization_barrier((kvl_w, ffn_shard))
    ffn_w = spread_two(ffn_shard, "fsdp", "ctx", 1)
    gain_one = kvl_w[:, low_at + rank].astype(f32)
    gain_two = kvl_w[:, low_at + rank + 1].astype(f32)

    facts, segrow = row_facts(lengths[0], row_count)
    up_pad = jnp.concatenate(
        [rank_up, jnp.zeros((LANES - rank, rank_up.shape[1]), bf16)], axis=0
    )
    bias_row = rank_bias.astype(f32)[None, :]
    gain_row = head_gain.astype(f32)[None, :]

    inputs = tokens.astype(f32)
    scale_one = rms_scale(inputs)
    normed = (inputs * scale_one * gain_one[None, :]).astype(bf16)
    proj = dot(normed, kvl_w, NN).astype(bf16)
    spans = row_count // SPAN
    pack_rows = HEAD_V + 16
    fpre, cum, run, local_states, packed = call(
        functools.partial(decay_kernel, heads, low_at),
        (
            shape_of(row_count, key_cols),
            shape_of(row_count, key_cols),
            shape_of(row_count, key_cols),
            shape_of(heads, spans + 1, HEAD_V, HEAD_K),
            shape_of(heads, pack_rows, HEAD_K, dtype=bf16),
        ),
    )(proj, up_pad, bias_row, facts)
    incoming = chained(packed, "ctx", False)
    query_gate = dot(normed, qg_w, NN)
    attended, mixed, states = call(
        functools.partial(forward_kernel, heads),
        (
            shape_of(row_count, value_cols, dtype=bf16),
            shape_of(row_count, value_cols),
            shape_of(heads, spans + 1, HEAD_V, HEAD_K, dtype=bf16),
        ),
    )(proj, query_gate, cum, facts, segrow, local_states, incoming, gain_row)
    attn_part = dot(attended, out_w, NT).astype(bf16)
    inputs_own = pick(tokens, tp_index, own_rows, 0).astype(f32)
    hidden_in = inputs_own + collect(attn_part, "tp", 0)

    scale_two = rms_scale(hidden_in)
    normed_two = spread(
        (hidden_in * scale_two * gain_two[None, :]).astype(bf16), "tp", 0
    )
    gate_val = dot(normed_two, ffn_w[0], NN)
    up_val = dot(normed_two, ffn_w[1], NN)
    gate_act = jax.nn.sigmoid(gate_val)
    hidden = (gate_val * gate_act * up_val).astype(bf16)
    hidden_grad = dot(cotangent, ffn_w[2], NN)
    gate_back = (hidden_grad * up_val * gate_act * (1.0 + gate_val * (1.0 - gate_act))).astype(
        bf16
    )
    up_back = (hidden_grad * gate_val * gate_act).astype(bf16)
    two_part = (dot(gate_back, ffn_w[0], NT) + dot(up_back, ffn_w[1], NT)).astype(bf16)
    two_grad = collect(two_part, "tp", 0)
    ffn_grads = jnp.stack(
        [
            dot(normed_two, gate_back, TN).astype(bf16),
            dot(normed_two, up_back, TN).astype(bf16),
            dot(cotangent, hidden, TN).astype(bf16),
        ],
        axis=0,
    )
    ffn_share = collect_two(ffn_grads, "fsdp", "ctx", 1)

    ffn_gain_part = jnp.sum(two_grad * hidden_in * scale_two, axis=0)
    weighted_two = two_grad * gain_two[None, :]
    cotangent_own = pick(cotangent, tp_index, own_rows, 0).astype(f32)
    hidden_in_grad = (
        cotangent_own
        + scale_two * weighted_two
        - hidden_in
        * scale_two**3
        * jnp.mean(weighted_two * hidden_in, axis=-1, keepdims=True)
    )
    residual_back = spread(hidden_in_grad.astype(bf16), "tp", 0)

    ffn_part = dot(hidden, ffn_w[2], NT).astype(bf16)
    ffn_part, residual_back = lax.optimization_barrier((ffn_part, residual_back))
    block_out = spread((hidden_in + collect(ffn_part, "tp", 0)).astype(bf16), "tp", 0)

    attended_grad = dot(residual_back, out_w, NN)
    mixed_grad, gate_pre_back, head_gain_part, grad_packed = call(
        functools.partial(gate_kernel, heads),
        (
            shape_of(row_count, value_cols, dtype=bf16),
            shape_of(row_count, value_cols, dtype=bf16),
            shape_of(1, HEAD_V),
            shape_of(heads, pack_rows, HEAD_K, dtype=bf16),
        ),
    )(attended_grad, query_gate, mixed, run, facts, gain_row)
    beyond = chained(grad_packed, "ctx", True)
    back_kvl, back_qg, bias_part, rank_up_part = call(
        lambda a, b, c, d, e, g, h, i, j, k, m, *outs: backward_kernel(
            heads, a, b, c, d, e, g, h, i, j, k, m, low_at, *outs
        ),
        (
            shape_of(row_count, low_at + LANES, dtype=bf16),
            shape_of(row_count, key_cols + value_cols, dtype=bf16),
            shape_of(1, key_cols),
            shape_of(LANES, key_cols),
        ),
        (pltpu.VMEM((spans, HEAD_V, HEAD_K), bf16),),
    )(
        proj,
        query_gate,
        cum,
        fpre,
        facts,
        segrow,
        states,
        mixed_grad,
        gate_pre_back,
        beyond,
        up_pad,
    )
    normed_part = (dot(back_kvl, kvl_w, NT) + dot(back_qg, qg_w, NT)).astype(bf16)
    normed_grad = collect(normed_part, "tp", 0)
    attn_grads = jnp.concatenate(
        [
            dot(normed, back_kvl, TN).astype(bf16),
            dot(normed, back_qg, TN).astype(bf16),
            dot(residual_back, attended, TN).astype(bf16),
        ],
        axis=1,
    )
    attn_share = collect_two(attn_grads, "fsdp", "ctx", 0)
    scale_own = pick(scale_one, tp_index, own_rows, 0)
    attn_gain_part = jnp.sum(normed_grad * inputs_own * scale_own, axis=0)
    weighted_one = normed_grad * gain_one[None, :]
    tokens_grad = spread(
        (
            hidden_in_grad
            + scale_own * weighted_one
            - inputs_own
            * scale_own**3
            * jnp.mean(weighted_one * inputs_own, axis=-1, keepdims=True)
        ).astype(bf16),
        "tp",
        0,
    ).astype(f32)

    over_all = jnp.concatenate([attn_gain_part, ffn_gain_part, head_gain_part[0]])
    over_rows = jnp.concatenate([rank_up_part[:rank].reshape(-1), bias_part.reshape(-1)])
    small = jnp.concatenate([over_all, over_rows]).reshape(-1, LANES)
    small = whole_sum(whole_sum(small, "fsdp"), "ctx")
    down_share = attn_share[:, low_at : low_at + LANES]
    top = over_all.shape[0] // LANES
    across = whole_sum(jnp.concatenate([small[:top], down_share], axis=0), "tp")
    sums = across[:top].reshape(-1)
    rank_down_grad = across[top:, :rank]
    flat = small[top:].reshape(-1)
    place = lax.axis_index("fsdp") * lax.axis_size("ctx") + lax.axis_index("ctx")
    qg_at = low_at + LANES
    out_at = qg_at + key_cols + value_cols
    return (
        block_out,
        tokens_grad,
        pick(sums[:width], place, shard, 0),
        attn_share[:, qg_at : qg_at + key_cols],
        attn_share[:, :key_cols],
        attn_share[:, key_cols:low_at],
        attn_share[:, qg_at + key_cols : out_at],
        rank_down_grad,
        flat[: rank * key_cols].reshape(rank, key_cols),
        flat[rank * key_cols :],
        sums[2 * width :],
        attn_share[:, out_at:].T,
        pick(sums[width : 2 * width], place, shard, 0),
        ffn_share[0],
        ffn_share[1],
        ffn_share[2].T,
    )


def solution(mesh):
    rows = P(("fsdp", "ctx"), None)
    vector = P(("fsdp", "ctx"))
    both = P(("fsdp", "ctx"), "tp")
    turned = P("tp", ("fsdp", "ctx"))
    return jax.shard_map(
        local,
        mesh=mesh,
        in_specs=(
            rows,
            rows,
            P("fsdp", None),
            vector,
            both,
            both,
            both,
            both,
            rows,
            P(None, "tp"),
            P("tp"),
            P(),
            turned,
            vector,
            both,
            both,
            turned,
        ),
        out_specs=(
            rows,
            rows,
            vector,
            both,
            both,
            both,
            both,
            rows,
            P(None, "tp"),
            P("tp"),
            P(),
            turned,
            vector,
            both,
            both,
            turned,
        ),
        check_vma=False,
    )
```

```python
import functools

import jax
import jax.numpy as jnp
from jax import lax
from jax.experimental import pallas as pl
from jax.experimental.pallas import tpu as pltpu
from jax.sharding import PartitionSpec as P


HEAD_K = 128
HEAD_V = 256
SPAN = 64
PAIR = 128
LANES = 128
epsilon = 1e-06
logit_scale = 16.0
bf16 = jnp.bfloat16
f32 = jnp.float32


def target(count, index, hop):
    return index ^ hop if count & (count - 1) == 0 else (index + hop) % count


def origin(count, index, hop):
    return index ^ hop if count & (count - 1) == 0 else (index - hop + count) % count


def swap(value, axis, hop):
    count = lax.axis_size(axis)
    return lax.ppermute(value, axis, [(i, target(count, i, hop)) for i in range(count)])


def pick(value, position, size, dim):
    return lax.dynamic_slice_in_dim(value, position * size, size, dim)


def block(shape, dim, start, size):
    return tuple(
        pl.ds(start, size) if at == dim else slice(None) for at in range(len(shape))
    )


def assemble_kernel(count, size, dim, places_ref, *refs):
    out_ref, sems = refs[count:]
    copies = []
    for piece in range(count):
        start = pl.multiple_of(places_ref[piece] * size, size)
        copies.append(
            pltpu.make_async_copy(
                refs[piece],
                out_ref.at[block(out_ref.shape, dim, start, size)],
                sems.at[piece],
            )
        )
    for copy in copies:
        copy.start()
    for copy in copies:
        copy.wait()


def widen_kernel(count, size, places_ref, *refs):
    out_ref = refs[count]
    for piece in range(count):
        start = pl.multiple_of(places_ref[piece] * size, size)
        out_ref[pl.ds(start, size), :] = refs[piece][...].astype(out_ref.dtype)


def assemble(pieces, places, dim, dtype):
    first = pieces[0]
    size, count = first.shape[dim], len(pieces)
    shape = first.shape[:dim] + (count * size,) + first.shape[dim + 1 :]
    out = jax.ShapeDtypeStruct(shape, dtype)
    if size % (LANES if dim == len(shape) - 1 else 16):
        full = jnp.zeros(shape, dtype)
        for piece, value in enumerate(pieces):
            full = lax.dynamic_update_slice_in_dim(
                full, value.astype(dtype), places[piece] * size, dim
            )
        return full
    if dtype != first.dtype:
        return call(functools.partial(widen_kernel, count, size), out, scalars=1)(
            places, *pieces
        )
    anywhere = pl.BlockSpec(memory_space=pltpu.HBM)
    return pl.pallas_call(
        functools.partial(assemble_kernel, count, size, dim),
        out_shape=out,
        in_specs=[pl.BlockSpec(memory_space=pltpu.SMEM)] + [anywhere] * count,
        out_specs=anywhere,
        scratch_shapes=[pltpu.SemaphoreType.DMA((count,))],
        compiler_params=pltpu.CompilerParams(vmem_limit_bytes=4 << 20),
    )(places, *pieces)


def around(axis):
    count, mine = lax.axis_size(axis), lax.axis_index(axis)
    return [origin(count, mine, hop) for hop in range(count)]


def numbers(values):
    return jnp.stack([jnp.asarray(value, jnp.int32) for value in values])


def pieces_of(value, axis):
    return [value] + [swap(value, axis, hop) for hop in range(1, lax.axis_size(axis))]


def gathered(value, axis):
    if lax.axis_size(axis) != 4:
        return pieces_of(value, axis)
    across = swap(value, axis, 2)
    both = jnp.stack([value, across])
    both = swap(both, axis, 1)
    return [value, both[0], across, both[1]]


def reduced(pieces, axis):
    if lax.axis_size(axis) != 4:
        return summed(pieces, axis)
    both = swap(jnp.stack([pieces[1], pieces[3]]), axis, 1).astype(f32)
    other = (pieces[2].astype(f32) + both[1]).astype(bf16)
    return pieces[0].astype(f32) + both[0] + swap(other, axis, 2).astype(f32)


def split_kernel(count, size, places_ref, value_ref, *out_refs):
    for piece in range(count):
        start = pl.multiple_of(places_ref[piece] * size, size)
        out_refs[piece][...] = value_ref[pl.ds(start, size), :]


def split(value, places):
    count = places.shape[0]
    size = value.shape[0] // count
    return call(
        functools.partial(split_kernel, count, size),
        tuple(
            jax.ShapeDtypeStruct((size, value.shape[1]), value.dtype) for _ in range(count)
        ),
        scalars=1,
    )(places, value)


def pass_on(near, axis):
    return [
        piece if step == 0 else swap(piece, axis, step)
        for piece in near
        for step in range(lax.axis_size(axis))
    ]


def places_two(outer, inner):
    return numbers(
        [
            row * lax.axis_size(inner) + column
            for column in around(inner)
            for row in around(outer)
        ]
    )


def collect(value, axis, dim, dtype):
    count, mine = lax.axis_size(axis), lax.axis_index(axis)
    size = value.shape[dim] // count
    pieces = [
        pick(value, target(count, mine, hop), size, dim) if hop else pick(value, mine, size, dim)
        for hop in range(count)
    ]
    pieces = [pieces[0]] + [swap(pieces[hop], axis, hop) for hop in range(1, count)]
    total = pieces[0].astype(f32)
    for piece in pieces[1:]:
        total = total + piece.astype(f32)
    return total.astype(dtype)


def summed(pieces, axis):
    total = pieces[0].astype(f32)
    for hop in range(1, lax.axis_size(axis)):
        total = total + swap(pieces[hop], axis, hop).astype(f32)
    return total


def shifted(value, axis, backward):
    count = lax.axis_size(axis)
    pieces = []
    for hop in range(1, count):
        pairs = [(i, i + hop) for i in range(count - hop)]
        if backward:
            pairs = [(b, a) for a, b in pairs]
        pieces.append(lax.ppermute(value, axis, pairs))
    return pieces


def sum_kernel(*refs):
    total = refs[0][...]
    for ref in refs[1:-1]:
        total = total + ref[...]
    refs[-1][...] = total


def whole_sum(value, axis):
    pieces = [value] + [swap(value, axis, hop) for hop in range(1, lax.axis_size(axis))]
    return call(sum_kernel, jax.ShapeDtypeStruct(value.shape, value.dtype))(*pieces)


def mark(value):
    return call(sum_kernel, jax.ShapeDtypeStruct(value.shape, value.dtype))(value)


NT = (((1,), (1,)), ((), ()))
NN = (((1,), (0,)), ((), ()))
TN = (((0,), (0,)), ((), ()))


def mm(left, right, dims):
    return lax.dot_general(
        left.astype(bf16), right.astype(bf16), dims, preferred_element_type=f32
    )


def pair_places():
    rows = lax.broadcasted_iota(jnp.int32, (PAIR, PAIR), 0)
    cols = lax.broadcasted_iota(jnp.int32, (PAIR, PAIR), 1)
    return rows, cols, (rows // SPAN) == (cols // SPAN)


def split_mm(ones, value):
    high = value.astype(bf16)
    rest = value - high.astype(f32)
    middle = rest.astype(bf16)
    low = (rest - middle.astype(f32)).astype(bf16)
    return mm(ones, high, NN) + mm(ones, middle, NN) + mm(ones, low, NN)


SEG, ENTER, TAIL, KEPT, OPEN, DEV_IN, _ = range(7)


def chained(pack_refs, head):
    value = None
    for ref in reversed(pack_refs):
        state = ref[head, :HEAD_V, :].astype(f32)
        if value is not None:
            state = state + ref[head, HEAD_V : HEAD_V + 1, :].astype(f32) * value
        value = state
    return jnp.zeros((HEAD_V, HEAD_K), f32) if value is None else value


def key_at(head):
    return slice(head * HEAD_K, (head + 1) * HEAD_K)


def value_at(head, start=0):
    return slice(start + head * HEAD_V, start + (head + 1) * HEAD_V)


def start_kernel(heads, count, shard, rank, places_ref, *refs):
    piece_refs = refs[:count]
    (
        tokens_ref,
        up_ref,
        bias_ref,
        facts_ref,
        w_ref,
        gains_ref,
        normed_ref,
        kvl_ref,
        decay_ref,
        state_ref,
        pack_ref,
        extra_ref,
        rt_ref,
        sems,
    ) = refs[count:]
    row_count = tokens_ref.shape[0]
    spans = row_count // SPAN
    key_cols = heads * HEAD_K
    both_cols = key_cols + heads * HEAD_V
    kv_ref, low_ref = kvl_ref.at[:, :both_cols], kvl_ref.at[:, both_cols:]
    cum_ref, run_ref, fpre_ref = decay_parts(decay_ref)
    extra = piece_refs[0].shape[0] - shard
    lanes = piece_refs[0].shape[1] // 2
    copies = []
    for piece, ref in enumerate(piece_refs):
        start = pl.multiple_of(places_ref[piece] * shard, shard)
        other = pl.multiple_of(places_ref[piece] * extra, extra)
        copies.append(
            pltpu.make_async_copy(
                ref.at[pl.ds(0, shard), :],
                w_ref.at[pl.ds(start, shard), pl.ds(0, 2 * lanes)],
                sems.at[0, piece],
            )
        )
        copies.append(
            pltpu.make_async_copy(
                ref.at[pl.ds(shard, extra), :],
                extra_ref.at[pl.ds(other, extra), :],
                sems.at[1, piece],
            )
        )
    for copy in copies:
        copy.start()
    for copy in copies:
        copy.wait()
    rt_ref[...] = jnp.zeros_like(rt_ref)
    gains_ref[...] = jnp.zeros_like(gains_ref)
    for place in range(count):
        at = slice(place * shard, (place + 1) * shard)
        rt_ref[:rank, at] = extra_ref[place * extra : place * extra + rank, :shard]
        gains_ref[0:2, at] = extra_ref[
            place * extra : place * extra + 2, lanes : lanes + shard
        ].astype(f32)
    w_ref[:, 2 * lanes :] = rt_ref[...].astype(f32).T.astype(bf16)
    inputs = tokens_ref[...].astype(f32)
    scale = lax.rsqrt(jnp.mean(inputs * inputs, axis=1, keepdims=True) + epsilon)
    normed = (inputs * scale * gains_ref[0:1, :]).astype(bf16)
    normed_ref[...] = normed
    kv_ref[...] = mm(normed, w_ref[:, : kv_ref.shape[1]], NN).astype(bf16)
    low_ref[...] = mm(normed, w_ref[:, 2 * lanes :], NN).astype(bf16)

    rows, cols, same = pair_places()
    lower = jnp.where(same & (rows >= cols), 1.0, 0.0).astype(bf16)
    fpre = mm(low_ref[...], up_ref[...], NN) + bias_ref[...]
    fpre_ref[...] = fpre
    log_decay = (jnp.minimum(fpre, 0.0) - jnp.log1p(jnp.exp(-jnp.abs(fpre)))) * (
        1.0 / logit_scale
    )
    for base in range(0, row_count, PAIR):
        cum_ref[base : base + PAIR, :] = split_mm(lower, log_decay[base : base + PAIR, :])
    for head in range(heads):
        at, vat = key_at(head), value_at(head, key_cols)
        state = jnp.zeros((HEAD_V, HEAD_K), f32)
        offset = jnp.zeros((1, HEAD_K), f32)
        for span in range(spans):
            here = slice(span * SPAN, (span + 1) * SPAN)
            first = slice(span * SPAN, span * SPAN + 1)
            cum = cum_ref[here, at]
            ending = cum[SPAN - 1 : SPAN, :]
            run_ref[here, at] = cum + offset
            offset = offset + ending
            tail = jnp.exp(ending - cum) * facts_ref[here, TAIL : TAIL + 1]
            fresh = mm(kv_ref[here, vat], kv_ref[here, at].astype(f32) * tail, TN)
            kept = jnp.exp(ending) * facts_ref[first, KEPT : KEPT + 1]
            state_ref[head, span] = state
            state = kept * state + fresh
        state_ref[head, spans] = state
        put_pack(pack_ref, head, state, offset, facts_ref)


def decay_parts(ref):
    width = ref.shape[1] // 3
    return tuple(ref.at[:, part * width : (part + 1) * width] for part in range(3))


def put_pack(pack_ref, head, state, total, facts_ref):
    row_count = facts_ref.shape[0]
    pack_ref[head, :HEAD_V, :] = state.astype(bf16)
    through = jnp.exp(total) * facts_ref[row_count - 1 : row_count, DEV_IN : DEV_IN + 1]
    pack_ref[head, HEAD_V:, :] = jnp.broadcast_to(
        through, (pack_ref.shape[1] - HEAD_V, HEAD_K)
    ).astype(bf16)


def inner_kernel(heads, normed_ref, w_ref, kvl_ref, decay_ref, facts_ref, segrow_ref, qg_ref, inner_ref, enter_ref):
    row_count = normed_ref.shape[0]
    key_cols = heads * HEAD_K
    rows, cols, same = pair_places()
    ordered = same & (rows >= cols)
    cum_ref = decay_parts(decay_ref)[0]
    split = kvl_ref.shape[1] - LANES
    kv_ref = kvl_ref.at[:, :split]
    qg_ref[...] = mm(normed_ref[...], w_ref[:, split : 2 * split], NN)
    for head in range(heads):
        at, vat = key_at(head), value_at(head, key_cols)
        for base in range(0, row_count, PAIR):
            here = slice(base, base + PAIR)
            cum = cum_ref[here, at]
            query = qg_ref[here, at].astype(bf16).astype(f32) * HEAD_K ** (-0.5)
            query_decayed = query * jnp.exp(cum)
            key_decayed = kv_ref[here, at].astype(f32) * jnp.exp(-cum)
            visible = ordered & (facts_ref[here, SEG : SEG + 1] == segrow_ref[:, here])
            scores = jnp.where(visible, mm(query_decayed, key_decayed, NT), 0.0)
            enter_ref[here, at] = (
                query_decayed * facts_ref[here, ENTER : ENTER + 1]
            ).astype(bf16)
            inner_ref[here, value_at(head)] = mm(scores, kv_ref[here, vat], NN)


def forward_kernel(heads, hops, *refs):
    pack_refs = refs[:hops]
    qg_ref, inner_ref, enter_ref, decay_ref, facts_ref, local_ref, gain_ref, att_ref, mixed_ref, state_ref = refs[hops:]
    row_count = qg_ref.shape[0]
    spans = row_count // SPAN
    cum_ref = decay_parts(decay_ref)[0]
    gain = gain_ref[...]
    for head in range(heads):
        at, out_at = key_at(head), value_at(head)
        gate_at = value_at(head, heads * HEAD_K)
        incoming = chained(pack_refs, head)
        product = jnp.ones((1, HEAD_K), f32)
        for span in range(spans):
            here = slice(span * SPAN, (span + 1) * SPAN)
            first = slice(span * SPAN, span * SPAN + 1)
            state = (local_ref[head, span] + product * incoming).astype(bf16)
            state_ref[head, span] = state
            ending = cum_ref[span * SPAN + SPAN - 1 : span * SPAN + SPAN, at]
            product = product * (jnp.exp(ending) * facts_ref[first, KEPT : KEPT + 1])
            mixed = inner_ref[here, out_at] + mm(enter_ref[here, at], state, NT)
            mixed_ref[here, out_at] = mixed
            scale = lax.rsqrt(jnp.mean(mixed * mixed, axis=1, keepdims=True) + epsilon)
            gate = qg_ref[here, gate_at]
            att_ref[here, out_at] = (
                mixed * scale * gain * (gate * jax.nn.sigmoid(gate))
            ).astype(bf16)
        state_ref[head, spans] = (local_ref[head, spans] + product * incoming).astype(bf16)


def gate_kernel(heads, count, own_rows, places_ref, *refs):
    agrad_refs = refs[:count]
    qg_ref, mixed_ref, decay_ref, facts_ref, gain_ref, mgrad_ref, gback_ref, hgain_ref, pack_ref = refs[count:]
    row_count = qg_ref.shape[0]
    run_ref = decay_parts(decay_ref)[1]
    gain = gain_ref[...]
    total = jnp.zeros((1, HEAD_V), f32)
    for head in range(heads):
        at, out_at = key_at(head), value_at(head)
        gate_at = value_at(head, heads * HEAD_K)
        state = jnp.zeros((HEAD_V, HEAD_K), f32)
        for piece in range(count):
            for base in range(0, own_rows, PAIR):
                here = pl.ds(
                    pl.multiple_of(places_ref[piece] * own_rows + base, PAIR), PAIR
                )
                mixed = mixed_ref[here, out_at]
                scale = lax.rsqrt(jnp.mean(mixed * mixed, axis=1, keepdims=True) + epsilon)
                unit = mixed * scale
                gate = qg_ref[here, gate_at]
                sig = jax.nn.sigmoid(gate)
                agrad = agrad_refs[piece][base : base + PAIR, out_at].astype(f32)
                gback_ref[here, out_at] = (
                    agrad * (unit * gain) * sig * (1.0 + gate * (1.0 - sig))
                ).astype(bf16)
                ugg = agrad * (gate * sig)
                total = total + jnp.sum(ugg * unit, axis=0, keepdims=True)
                ug = ugg * gain
                mgrad = (
                    scale * (ug - unit * jnp.mean(ug * unit, axis=1, keepdims=True))
                ).astype(bf16)
                mgrad_ref[here, out_at] = mgrad
                query = qg_ref[here, at].astype(bf16).astype(f32) * HEAD_K ** (-0.5)
                lifted = (
                    query * jnp.exp(run_ref[here, at]) * facts_ref[here, DEV_IN : DEV_IN + 1]
                )
                state = state + mm(mgrad, lifted, TN)
        put_pack(pack_ref, head, state, run_ref[row_count - 1 : row_count, at], facts_ref)
    hgain_ref[...] = total


def backward_kernel(heads, hops, *refs):
    pack_refs = refs[:hops]
    kvl_ref, qg_ref, decay_ref, facts_ref, segrow_ref, state_ref, mgrad_ref, gback_ref, up_ref = refs[hops : hops + 9]
    back_ref, bias_ref, rup_ref, after_ref, rank_ref = refs[hops + 9 :]
    query_from = kvl_ref.shape[1] - LANES
    kv_ref, low_ref = kvl_ref.at[:, :query_from], kvl_ref.at[:, query_from:]
    cum_ref, _, fpre_ref = decay_parts(decay_ref)
    rank_from = 2 * query_from
    row_count = kv_ref.shape[0]
    spans = row_count // SPAN
    key_cols = heads * HEAD_K
    rows, cols, same = pair_places()
    ordered = same & (rows >= cols)
    upper = jnp.where(same & (cols >= rows), 1.0, 0.0)
    for head in range(heads):
        at, vat, out_at = key_at(head), value_at(head, key_cols), value_at(head)
        after = chained(pack_refs, head)
        for span in reversed(range(spans)):
            here = slice(span * SPAN, (span + 1) * SPAN)
            first = slice(span * SPAN, span * SPAN + 1)
            cum = cum_ref[here, at]
            after_ref[span] = after.astype(bf16)
            query = qg_ref[here, at].astype(bf16).astype(f32) * HEAD_K ** (-0.5)
            entering = query * jnp.exp(cum) * facts_ref[here, ENTER : ENTER + 1]
            kept = jnp.exp(cum[SPAN - 1 : SPAN, :]) * facts_ref[first, KEPT : KEPT + 1]
            after = kept * after + mm(mgrad_ref[here, out_at], entering, TN)
        bias = jnp.zeros((1, HEAD_K), f32)
        rup = jnp.zeros((LANES, HEAD_K), f32)
        for base in range(0, row_count, PAIR):
            here = slice(base, base + PAIR)
            cum = cum_ref[here, at]
            query = qg_ref[here, at].astype(bf16).astype(f32) * HEAD_K ** (-0.5)
            key = kv_ref[here, at].astype(f32)
            value = kv_ref[here, vat]
            mgrad = mgrad_ref[here, out_at]
            grow = jnp.exp(cum)
            shrink = jnp.exp(-cum)
            query_decayed = (query * grow).astype(bf16)
            key_decayed = (key * shrink).astype(bf16)
            segment = facts_ref[here, SEG : SEG + 1]
            visible = ordered & (segment == segrow_ref[:, here])
            scores = jnp.where(visible, mm(query_decayed, key_decayed, NT), 0.0).astype(bf16)
            dscore = jnp.where(visible, mm(mgrad, value, NT), 0.0).astype(bf16)
            dquery_in = mm(dscore, key_decayed, NN)
            dkey_in = mm(dscore, query_decayed, TN)
            dvalue_in = mm(scores, mgrad, TN)
            terms, carries = [], []
            for half in range(PAIR // SPAN):
                mine = slice(half * SPAN, (half + 1) * SPAN)
                span = base // SPAN + half
                place = slice(span * SPAN, (span + 1) * SPAN)
                state = state_ref[head, span]
                behind = after_ref[span]
                ending = cum[(half + 1) * SPAN - 1 : (half + 1) * SPAN, :]
                tail = jnp.exp(ending - cum[mine, :]) * facts_ref[place, TAIL : TAIL + 1]
                lifted = grow[mine, :] * facts_ref[place, ENTER : ENTER + 1]
                dquery = grow[mine, :] * dquery_in[mine, :] + lifted * mm(
                    mgrad[mine, :], state, NN
                )
                dkey = shrink[mine, :] * dkey_in[mine, :] + tail * mm(
                    value[mine, :], behind, NN
                )
                dvalue = dvalue_in[mine, :] + mm(key[mine, :] * tail, behind, NT)
                back_ref[
                    place, query_from + head * HEAD_K : query_from + (head + 1) * HEAD_K
                ] = (dquery * HEAD_K ** (-0.5)).astype(bf16)
                back_ref[place, at] = dkey.astype(bf16)
                back_ref[place, vat] = dvalue.astype(bf16)
                terms.append(query[mine, :] * dquery - key[mine, :] * dkey)
                carry = jnp.sum(
                    state_ref[head, span + 1].astype(f32) * behind.astype(f32),
                    axis=0,
                    keepdims=True,
                )
                carries.append(facts_ref[place, TAIL : TAIL + 1] * carry)
            later = jnp.where(segment == segrow_ref[:, here], upper, 0.0).astype(bf16)
            decay_grad = split_mm(later, jnp.concatenate(terms, axis=0)) + jnp.concatenate(
                carries, axis=0
            )
            decay_grad = jnp.where(facts_ref[here, OPEN : OPEN + 1] > 0.0, 0.0, decay_grad)
            fgrad = decay_grad * jax.nn.sigmoid(-fpre_ref[here, at]) * (1.0 / logit_scale)
            bias = bias + jnp.sum(fgrad, axis=0, keepdims=True)
            fback = fgrad.astype(bf16)
            rup = rup + mm(low_ref[here, :], fback, TN)
            rank = mm(fback, up_ref[:, at], NT)
            if head > 0:
                rank = rank + rank_ref[here, :]
            rank_ref[here, :] = rank
        bias_ref[:, at] = bias
        rup_ref[:, at] = rup
    back_ref[:, rank_from:] = rank_ref[...].astype(bf16)
    back_ref[:, query_from + key_cols : rank_from] = gback_ref[...]


def call(kernel, outs, scratch=(), scalars=0, anywhere=0):
    def run(*args):
        specs = {}
        if scalars:
            specs["in_specs"] = [pl.BlockSpec(memory_space=pltpu.SMEM)] * scalars
            specs["in_specs"] += [pl.BlockSpec(memory_space=pltpu.HBM)] * anywhere
            specs["in_specs"] += [pl.BlockSpec()] * (len(args) - scalars - anywhere)
        return pl.pallas_call(
            kernel,
            out_shape=outs,
            scratch_shapes=list(scratch),
            compiler_params=pltpu.CompilerParams(vmem_limit_bytes=48 << 20),
            **specs,
        )(*args)

    return run


def shape_of(*dims, dtype=f32):
    return jax.ShapeDtypeStruct(dims, dtype)


def row_facts(length_row, row_count):
    seq_ends = jnp.cumsum(length_row)
    seq_starts = seq_ends - length_row
    ctx_index = lax.axis_index("ctx")
    first = ctx_index * row_count
    positions = first + jnp.arange(row_count, dtype=jnp.int32)

    def label(places):
        return jnp.sum(
            (places[:, None] >= seq_ends[None, :]).astype(jnp.int32), axis=1
        ).astype(jnp.int32)

    segment = label(positions)
    spans = row_count // SPAN
    span_first = first + jnp.arange(spans, dtype=jnp.int32) * SPAN
    before = jnp.where(span_first > 0, label(span_first - 1), -1)
    last = label(span_first + SPAN - 1)
    opening = jnp.any(positions[:, None] == seq_starts[None, :], axis=1)

    def wide(values):
        return jnp.repeat(values, SPAN)

    columns = (
        segment,
        segment == wide(before),
        segment == wide(last),
        wide(last == before),
        opening,
        segment == before[0],
        segment == last[-1],
        jnp.zeros_like(segment),
    )
    facts = jnp.stack([column.astype(f32) for column in columns], axis=1)
    return facts, segment.astype(f32)[None, :]


def rms_scale(field_in):
    return lax.rsqrt(jnp.mean(field_in * field_in, axis=-1, keepdims=True) + epsilon)


def dot(left, right, dims):
    return lax.dot_general(left, right, dims, preferred_element_type=f32)


def local(
    tokens,
    cotangent,
    lengths,
    attn_gain,
    query_proj,
    key_proj,
    value_proj,
    gate_proj,
    rank_down,
    rank_up,
    rank_bias,
    head_gain,
    output_proj,
    ffn_gain,
    ffn_gate,
    ffn_up,
    ffn_down,
):
    row_count, width = tokens.shape
    tp_count, tp_index = lax.axis_size("tp"), lax.axis_index("tp")
    own_rows = row_count // tp_count
    heads = query_proj.shape[1] // HEAD_K
    key_cols, value_cols = heads * HEAD_K, heads * HEAD_V
    both_cols = key_cols + value_cols
    shard, rank = rank_down.shape
    hops = lax.axis_size("ctx") - 1
    tp_places = numbers(around("tp"))
    row_places = places_two("fsdp", "ctx")
    count = row_places.shape[0]

    extra = -(-rank // 16) * 16
    lanes = both_cols

    def padded(values, rows, cols):
        return jnp.pad(values, ((0, rows - values.shape[0]), (0, cols - values.shape[1])))

    first = jnp.concatenate(
        [
            jnp.concatenate([key_proj, value_proj, query_proj, gate_proj], axis=1),
            jnp.concatenate(
                [
                    padded(rank_down.T, extra, lanes),
                    padded(jnp.stack([attn_gain, ffn_gain]), extra, lanes),
                ],
                axis=1,
            ),
        ],
        axis=0,
    )
    first_pieces = pass_on(pieces_of(first, "ctx"), "fsdp")
    out_shard = jnp.stack(pieces_of(output_proj, "tp"), axis=0)
    down_w = assemble(pass_on(pieces_of(ffn_down, "ctx"), "fsdp"), row_places, 1, bf16)

    facts, segrow = row_facts(lengths[0], row_count)
    up_pad = jnp.concatenate(
        [rank_up, jnp.zeros((LANES - rank, rank_up.shape[1]), bf16)], axis=0
    )
    bias_row = rank_bias.astype(f32)[None, :]
    gain_row = head_gain.astype(f32)[None, :]

    spans = row_count // SPAN
    pack_rows = HEAD_V + 16
    w, gains, normed, kvl, decays, local_states, packed = call(
        functools.partial(start_kernel, heads, count, shard, rank),
        (
            shape_of(width, 2 * both_cols + LANES, dtype=bf16),
            shape_of(8, width),
            shape_of(row_count, width, dtype=bf16),
            shape_of(row_count, both_cols + LANES, dtype=bf16),
            shape_of(row_count, 3 * key_cols),
            shape_of(heads, spans + 1, HEAD_V, HEAD_K),
            shape_of(heads, pack_rows, HEAD_K, dtype=bf16),
        ),
        (
            pltpu.VMEM((count * extra, 2 * both_cols), bf16),
            pltpu.VMEM((LANES, width), bf16),
            pltpu.SemaphoreType.DMA((2, count)),
        ),
        scalars=1,
        anywhere=count,
    )(row_places, *first_pieces, tokens, up_pad, bias_row, facts)
    packs = shifted(packed, "ctx", False)
    query_gate, inner, entering = call(
        functools.partial(inner_kernel, heads),
        (
            shape_of(row_count, both_cols),
            shape_of(row_count, value_cols),
            shape_of(row_count, key_cols, dtype=bf16),
        ),
    )(normed, w, kvl, decays, facts, segrow)
    out_near = pieces_of(out_shard, "ctx")
    out_w = assemble(pass_on(out_near, "fsdp"), row_places, 2, bf16)
    attended, mixed, states = call(
        functools.partial(forward_kernel, heads, hops),
        (
            shape_of(row_count, value_cols, dtype=bf16),
            shape_of(row_count, value_cols),
            shape_of(heads, spans + 1, HEAD_V, HEAD_K, dtype=bf16),
        ),
    )(*packs, query_gate, inner, entering, decays, facts, local_states, gain_row)
    att_pieces = pieces_of(attended, "tp")
    ffn_w = assemble(
        pass_on(pieces_of(jnp.stack([ffn_gate.T, ffn_up.T], axis=0), "ctx"), "fsdp"),
        row_places,
        2,
        bf16,
    )
    inputs = tokens.astype(f32)
    hidden_full = inputs
    for hop in range(tp_count):
        hidden_full = hidden_full + dot(att_pieces[hop], out_w[hop], NN)
    gain_two = gains[1:2]

    scale_two_full = rms_scale(hidden_full)
    normed_two = (hidden_full * scale_two_full * gain_two).astype(bf16)
    gate_val = dot(normed_two, ffn_w[0], NT)
    up_val = dot(normed_two, ffn_w[1], NT)
    gate_act = jax.nn.sigmoid(gate_val)
    hidden = (gate_val * gate_act * up_val).astype(bf16)
    hidden_grad = dot(cotangent, down_w, NT)
    gate_back = (hidden_grad * up_val * gate_act * (1.0 + gate_val * (1.0 - gate_act))).astype(
        bf16
    )
    up_back = (hidden_grad * gate_val * gate_act).astype(bf16)
    two_part = (dot(gate_back, ffn_w[0], NN) + dot(up_back, ffn_w[1], NN)).astype(bf16)
    two_pieces = split(two_part, tp_places)
    two_grad = summed(two_pieces, "tp")
    normed_two, gate_back, up_back, hidden, *_ = lax.optimization_barrier(
        (normed_two, gate_back, up_back, hidden, *two_pieces)
    )
    ffn_grads = jnp.stack(
        [
            dot(gate_back, normed_two, TN).astype(bf16),
            dot(up_back, normed_two, TN).astype(bf16),
            dot(hidden, cotangent, TN).astype(bf16),
        ],
        axis=0,
    )
    ffn_chip = collect(ffn_grads, "fsdp", 2, bf16)
    ffn_share = collect(ffn_chip, "ctx", 2, f32)
    ffn_part = dot(hidden, down_w, NN).astype(bf16)
    ffn_pieces = split(ffn_part, tp_places)

    hidden_in = pick(hidden_full, tp_index, own_rows, 0)
    scale_two = pick(scale_two_full, tp_index, own_rows, 0)
    ffn_gain_part = jnp.sum(two_grad * hidden_in * scale_two, axis=0)
    weighted_two = two_grad * gain_two
    cotangent_own = pick(cotangent, tp_index, own_rows, 0).astype(f32)
    hidden_in_grad = (
        cotangent_own
        + scale_two * weighted_two
        - hidden_in
        * scale_two**3
        * jnp.mean(weighted_two * hidden_in, axis=-1, keepdims=True)
    )
    residual_back = hidden_in_grad.astype(bf16)

    grad_pieces = [
        dot(residual_back, out_w[hop], NT).astype(bf16) for hop in range(tp_count)
    ]
    residual_later, hidden_block, *_ = lax.optimization_barrier(
        (residual_back, hidden_in, *grad_pieces)
    )
    grad_pieces = [grad_pieces[0]] + [
        swap(grad_pieces[hop], "tp", hop) for hop in range(1, tp_count)
    ]
    mixed_grad, gate_pre_back, head_gain_part, grad_packed = call(
        functools.partial(gate_kernel, heads, tp_count, own_rows),
        (
            shape_of(row_count, value_cols, dtype=bf16),
            shape_of(row_count, value_cols, dtype=bf16),
            shape_of(1, HEAD_V),
            shape_of(heads, pack_rows, HEAD_K, dtype=bf16),
        ),
        scalars=1,
    )(tp_places, *grad_pieces, query_gate, mixed, decays, facts, gain_row)
    grad_packs = shifted(grad_packed, "ctx", True)
    back, bias_part, rank_up_part = call(
        functools.partial(backward_kernel, heads, hops),
        (
            shape_of(row_count, 2 * both_cols + LANES, dtype=bf16),
            shape_of(1, key_cols),
            shape_of(LANES, key_cols),
        ),
        (
            pltpu.VMEM((spans, HEAD_V, HEAD_K), bf16),
            pltpu.VMEM((row_count, LANES), f32),
        ),
    )(
        *grad_packs,
        kvl,
        query_gate,
        decays,
        facts,
        segrow,
        states,
        mixed_grad,
        gate_pre_back,
        up_pad,
    )
    normed_pieces = split(dot(back, w, NT).astype(bf16), tp_places)
    normed_grad = summed(normed_pieces, "tp")
    back, *_ = lax.optimization_barrier((back, *normed_pieces))

    block_sum = reduced(ffn_pieces, "tp")
    block_own = (hidden_block + block_sum).astype(bf16)
    block_out = assemble(
        gathered(block_own, "tp"),
        tp_places,
        0,
        bf16,
    )

    output_grads = jnp.stack(
        [
            dot(pick(piece, tp_index, own_rows, 0), residual_later, TN).astype(bf16)
            for piece in att_pieces
        ],
        axis=0,
    )
    output_chip = collect(output_grads, "fsdp", 2, bf16)
    output_share = collect(output_chip, "ctx", 2, f32)
    attn_grads = dot(normed, back, TN).astype(bf16)
    attn_chip = collect(attn_grads, "fsdp", 0, bf16)
    attn_share = collect(attn_chip, "ctx", 0, f32)

    inputs_own = pick(tokens, tp_index, own_rows, 0).astype(f32)
    scale_own = rms_scale(inputs_own)
    attn_gain_part = jnp.sum(normed_grad * inputs_own * scale_own, axis=0)
    weighted_one = normed_grad * mark(gains)[0:1]
    tokens_own = (
        hidden_in_grad
        + scale_own * weighted_one
        - inputs_own
        * scale_own**3
        * jnp.mean(weighted_one * inputs_own, axis=-1, keepdims=True)
    ).astype(bf16)
    tokens_grad = assemble(gathered(tokens_own, "tp"), tp_places, 0, f32)

    over_all = jnp.concatenate([attn_gain_part, ffn_gain_part, head_gain_part[0]])
    over_rows = jnp.concatenate([rank_up_part[:rank].reshape(-1), bias_part.reshape(-1)])
    small = jnp.concatenate([over_all, over_rows]).reshape(-1, LANES)
    top = over_all.shape[0] // LANES
    small = whole_sum(whole_sum(small, "fsdp"), "ctx")
    flat = small[top:].reshape(-1)

    both_sums = jnp.concatenate(
        [attn_share[:, 2 * both_cols :], small[:top], jnp.zeros((-(top + shard) % 16, LANES), f32)],
        axis=0,
    ).astype(bf16)
    lasts = [
        jnp.concatenate(
            [
                output_share[hop].astype(bf16).reshape(-1, LANES)
                if shard % LANES == 0
                else jnp.pad(output_share[hop], ((0, 0), (0, LANES - shard))).astype(bf16),
                both_sums,
            ],
            axis=0,
        )
        for hop in range(tp_count)
    ]
    last = summed(lasts, "tp")
    output_grad = last[:value_cols, :shard]
    rank_down_grad = last[value_cols : value_cols + shard, :rank]
    sums = last[value_cols + shard : value_cols + shard + top].reshape(-1)
    place = lax.axis_index("fsdp") * lax.axis_size("ctx") + lax.axis_index("ctx")
    return (
        block_out,
        tokens_grad,
        pick(sums[:width], place, shard, 0),
        attn_share[:, both_cols : both_cols + key_cols],
        attn_share[:, :key_cols],
        attn_share[:, key_cols:both_cols],
        attn_share[:, both_cols + key_cols : 2 * both_cols],
        rank_down_grad,
        flat[: rank * key_cols].reshape(rank, key_cols),
        flat[rank * key_cols :],
        sums[2 * width :],
        output_grad,
        pick(sums[width : 2 * width], place, shard, 0),
        ffn_share[0].T,
        ffn_share[1].T,
        ffn_share[2],
    )


def solution(mesh):
    rows = P(("fsdp", "ctx"), None)
    vector = P(("fsdp", "ctx"))
    both = P(("fsdp", "ctx"), "tp")
    turned = P("tp", ("fsdp", "ctx"))
    return jax.shard_map(
        local,
        mesh=mesh,
        in_specs=(
            rows,
            rows,
            P("fsdp", None),
            vector,
            both,
            both,
            both,
            both,
            rows,
            P(None, "tp"),
            P("tp"),
            P(),
            turned,
            vector,
            both,
            both,
            turned,
        ),
        out_specs=(
            rows,
            rows,
            vector,
            both,
            both,
            both,
            both,
            rows,
            P(None, "tp"),
            P("tp"),
            P(),
            turned,
            vector,
            both,
            both,
            turned,
        ),
        check_vma=False,
    )
```

```python
import functools

import jax
import jax.numpy as jnp
from jax import lax
from jax.experimental import pallas as pl
from jax.experimental.pallas import tpu as pltpu
from jax.sharding import PartitionSpec as P


HEAD_K = 128
HEAD_V = 256
SPAN = 64
PAIR = 128
LANES = 128
epsilon = 1e-06
logit_scale = 16.0
bf16 = jnp.bfloat16
f32 = jnp.float32


def target(count, index, hop):
    return index ^ hop if count & (count - 1) == 0 else (index + hop) % count


def origin(count, index, hop):
    return index ^ hop if count & (count - 1) == 0 else (index - hop + count) % count


def swap(value, axis, hop):
    count = lax.axis_size(axis)
    return lax.ppermute(value, axis, [(i, target(count, i, hop)) for i in range(count)])


def pick(value, position, size, dim):
    return lax.dynamic_slice_in_dim(value, position * size, size, dim)


def block(shape, dim, start, size):
    return tuple(
        pl.ds(start, size) if at == dim else slice(None) for at in range(len(shape))
    )


def assemble_kernel(count, size, dim, places_ref, *refs):
    out_ref, sems = refs[count:]
    copies = []
    for piece in range(count):
        start = pl.multiple_of(places_ref[piece] * size, size)
        copies.append(
            pltpu.make_async_copy(
                refs[piece],
                out_ref.at[block(out_ref.shape, dim, start, size)],
                sems.at[piece],
            )
        )
    for copy in copies:
        copy.start()
    for copy in copies:
        copy.wait()


def widen_kernel(count, size, places_ref, *refs):
    out_ref = refs[count]
    for piece in range(count):
        start = pl.multiple_of(places_ref[piece] * size, size)
        out_ref[pl.ds(start, size), :] = refs[piece][...].astype(out_ref.dtype)


def assemble(pieces, places, dim, dtype, through=False):
    first = pieces[0]
    size, count = first.shape[dim], len(pieces)
    shape = first.shape[:dim] + (count * size,) + first.shape[dim + 1 :]
    out = jax.ShapeDtypeStruct(shape, dtype)
    if size % (LANES if dim == len(shape) - 1 else 16):
        full = jnp.zeros(shape, dtype)
        for piece, value in enumerate(pieces):
            full = lax.dynamic_update_slice_in_dim(
                full, value.astype(dtype), places[piece] * size, dim
            )
        return full
    if through:
        return call(functools.partial(widen_kernel, count, size), out, scalars=1)(
            places, *pieces
        )
    anywhere = pl.BlockSpec(memory_space=pltpu.HBM)
    return pl.pallas_call(
        functools.partial(assemble_kernel, count, size, dim),
        out_shape=out,
        in_specs=[pl.BlockSpec(memory_space=pltpu.SMEM)] + [anywhere] * count,
        out_specs=anywhere,
        scratch_shapes=[pltpu.SemaphoreType.DMA((count,))],
        compiler_params=pltpu.CompilerParams(vmem_limit_bytes=4 << 20),
    )(places, *[outside(piece) for piece in pieces])


def outside(value):
    return pltpu.with_memory_space_constraint(value, pltpu.HBM)


def around(axis):
    count, mine = lax.axis_size(axis), lax.axis_index(axis)
    return [origin(count, mine, hop) for hop in range(count)]


def numbers(values):
    return jnp.stack([jnp.asarray(value, jnp.int32) for value in values])


def pieces_of(value, axis):
    return [value] + [swap(value, axis, hop) for hop in range(1, lax.axis_size(axis))]


def gathered(value, axis):
    if lax.axis_size(axis) != 4:
        return pieces_of(value, axis)
    across = swap(value, axis, 2)
    both = jnp.stack([value, across])
    both = swap(both, axis, 1)
    return [value, both[0], across, both[1]]


def reduced(value, places, axis):
    paired = lax.axis_size(axis) == 4
    pieces = split(value, places, paired)
    if not paired:
        return summed(pieces, axis)
    own, beside, across = pieces
    both = swap(beside, axis, 1)
    other = (across.astype(f32) + both[1].astype(f32)).astype(bf16)
    return own.astype(f32) + both[0].astype(f32) + swap(other, axis, 2).astype(f32)


def split_kernel(count, size, paired, places_ref, value_ref, *out_refs):
    for piece in range(count):
        start = pl.multiple_of(places_ref[piece] * size, size)
        rows = value_ref[pl.ds(start, size), :]
        if paired and piece % 2:
            out_refs[1][piece // 2] = rows
        else:
            out_refs[piece][...] = rows


def split(value, places, paired=False):
    count = places.shape[0]
    size = value.shape[0] // count
    single = jax.ShapeDtypeStruct((size, value.shape[1]), value.dtype)
    outs = (single,) * count
    if paired:
        outs = (single, jax.ShapeDtypeStruct((2, *single.shape), value.dtype), single)
    return call(
        functools.partial(split_kernel, count, size, paired), outs, scalars=1
    )(places, value)


def pass_on(near, axis):
    return [
        piece if step == 0 else swap(piece, axis, step)
        for piece in near
        for step in range(lax.axis_size(axis))
    ]


def places_two(outer, inner):
    return numbers(
        [
            row * lax.axis_size(inner) + column
            for column in around(inner)
            for row in around(outer)
        ]
    )


def collect(value, axis, dim, dtype):
    count, mine = lax.axis_size(axis), lax.axis_index(axis)
    size = value.shape[dim] // count
    pieces = [
        pick(value, target(count, mine, hop), size, dim) if hop else pick(value, mine, size, dim)
        for hop in range(count)
    ]
    pieces = [pieces[0]] + [swap(pieces[hop], axis, hop) for hop in range(1, count)]
    total = pieces[0].astype(f32)
    for piece in pieces[1:]:
        total = total + piece.astype(f32)
    return total.astype(dtype)


def summed(pieces, axis):
    total = pieces[0].astype(f32)
    for hop in range(1, lax.axis_size(axis)):
        total = total + swap(pieces[hop], axis, hop).astype(f32)
    return total


def shifted(value, axis, backward):
    count = lax.axis_size(axis)
    pieces = []
    for hop in range(1, count):
        pairs = [(i, i + hop) for i in range(count - hop)]
        if backward:
            pairs = [(b, a) for a, b in pairs]
        pieces.append(lax.ppermute(value, axis, pairs))
    return pieces


def sum_kernel(*refs):
    total = refs[0][...]
    for ref in refs[1:-1]:
        total = total + ref[...]
    refs[-1][...] = total


def whole_sum(value, axis):
    pieces = [value] + [swap(value, axis, hop) for hop in range(1, lax.axis_size(axis))]
    return call(sum_kernel, jax.ShapeDtypeStruct(value.shape, value.dtype))(*pieces)


def mark(value):
    return call(sum_kernel, jax.ShapeDtypeStruct(value.shape, value.dtype))(value)


NT = (((1,), (1,)), ((), ()))
NN = (((1,), (0,)), ((), ()))
TN = (((0,), (0,)), ((), ()))


def mm(left, right, dims):
    return lax.dot_general(
        left.astype(bf16), right.astype(bf16), dims, preferred_element_type=f32
    )


def pair_places():
    rows = lax.broadcasted_iota(jnp.int32, (PAIR, PAIR), 0)
    cols = lax.broadcasted_iota(jnp.int32, (PAIR, PAIR), 1)
    return rows, cols, (rows // SPAN) == (cols // SPAN)


def split_mm(ones, value):
    high = value.astype(bf16)
    rest = value - high.astype(f32)
    middle = rest.astype(bf16)
    low = (rest - middle.astype(f32)).astype(bf16)
    return mm(ones, high, NN) + mm(ones, middle, NN) + mm(ones, low, NN)


SEG, ENTER, TAIL, KEPT, OPEN, DEV_IN, _ = range(7)


def chained(pack_refs, head):
    value = None
    for ref in reversed(pack_refs):
        state = ref[head, :HEAD_V, :].astype(f32)
        if value is not None:
            state = state + ref[head, HEAD_V : HEAD_V + 1, :].astype(f32) * value
        value = state
    return jnp.zeros((HEAD_V, HEAD_K), f32) if value is None else value


def key_at(head):
    return slice(head * HEAD_K, (head + 1) * HEAD_K)


def value_at(head, start=0):
    return slice(start + head * HEAD_V, start + (head + 1) * HEAD_V)


def start_kernel(heads, count, shard, rank, places_ref, *refs):
    piece_refs = refs[:count]
    (
        tokens_ref,
        up_ref,
        bias_ref,
        facts_ref,
        w_ref,
        gains_ref,
        normed_ref,
        kvl_ref,
        decay_ref,
        state_ref,
        pack_ref,
        extra_ref,
        rt_ref,
        sems,
    ) = refs[count:]
    row_count = tokens_ref.shape[0]
    spans = row_count // SPAN
    key_cols = heads * HEAD_K
    both_cols = key_cols + heads * HEAD_V
    kv_ref, low_ref = kvl_ref.at[:, :both_cols], kvl_ref.at[:, both_cols:]
    cum_ref, run_ref, fpre_ref = decay_parts(decay_ref)
    extra = piece_refs[0].shape[0] - shard
    lanes = piece_refs[0].shape[1] // 2
    copies = []
    for piece, ref in enumerate(piece_refs):
        start = pl.multiple_of(places_ref[piece] * shard, shard)
        other = pl.multiple_of(places_ref[piece] * extra, extra)
        copies.append(
            pltpu.make_async_copy(
                ref.at[pl.ds(0, shard), :],
                w_ref.at[pl.ds(start, shard), pl.ds(0, 2 * lanes)],
                sems.at[0, piece],
            )
        )
        copies.append(
            pltpu.make_async_copy(
                ref.at[pl.ds(shard, extra), :],
                extra_ref.at[pl.ds(other, extra), :],
                sems.at[1, piece],
            )
        )
    for copy in copies:
        copy.start()
    for copy in copies:
        copy.wait()
    rt_ref[...] = jnp.zeros_like(rt_ref)
    gains_ref[...] = jnp.zeros_like(gains_ref)
    for place in range(count):
        at = slice(place * shard, (place + 1) * shard)
        rt_ref[:rank, at] = extra_ref[place * extra : place * extra + rank, :shard]
        gains_ref[0:2, at] = extra_ref[
            place * extra : place * extra + 2, lanes : lanes + shard
        ].astype(f32)
    w_ref[:, 2 * lanes :] = rt_ref[...].astype(f32).T.astype(bf16)
    inputs = tokens_ref[...].astype(f32)
    scale = lax.rsqrt(jnp.mean(inputs * inputs, axis=1, keepdims=True) + epsilon)
    normed = (inputs * scale * gains_ref[0:1, :]).astype(bf16)
    normed_ref[...] = normed
    kv_ref[...] = mm(normed, w_ref[:, : kv_ref.shape[1]], NN).astype(bf16)
    low_ref[...] = mm(normed, w_ref[:, 2 * lanes :], NN).astype(bf16)

    rows, cols, same = pair_places()
    lower = jnp.where(same & (rows >= cols), 1.0, 0.0).astype(bf16)
    fpre = mm(low_ref[...], up_ref[...], NN) + bias_ref[...]
    fpre_ref[...] = fpre
    log_decay = (jnp.minimum(fpre, 0.0) - jnp.log1p(jnp.exp(-jnp.abs(fpre)))) * (
        1.0 / logit_scale
    )
    for base in range(0, row_count, PAIR):
        cum_ref[base : base + PAIR, :] = split_mm(lower, log_decay[base : base + PAIR, :])
    for head in range(heads):
        at, vat = key_at(head), value_at(head, key_cols)
        state = jnp.zeros((HEAD_V, HEAD_K), f32)
        offset = jnp.zeros((1, HEAD_K), f32)
        for span in range(spans):
            here = slice(span * SPAN, (span + 1) * SPAN)
            first = slice(span * SPAN, span * SPAN + 1)
            cum = cum_ref[here, at]
            ending = cum[SPAN - 1 : SPAN, :]
            run_ref[here, at] = cum + offset
            offset = offset + ending
            tail = jnp.exp(ending - cum) * facts_ref[here, TAIL : TAIL + 1]
            fresh = mm(kv_ref[here, vat], kv_ref[here, at].astype(f32) * tail, TN)
            kept = jnp.exp(ending) * facts_ref[first, KEPT : KEPT + 1]
            state_ref[head, span] = state
            state = kept * state + fresh
        state_ref[head, spans] = state
        put_pack(pack_ref, head, state, offset, facts_ref)


def decay_parts(ref):
    width = ref.shape[1] // 3
    return tuple(ref.at[:, part * width : (part + 1) * width] for part in range(3))


def put_pack(pack_ref, head, state, total, facts_ref):
    row_count = facts_ref.shape[0]
    pack_ref[head, :HEAD_V, :] = state.astype(bf16)
    through = jnp.exp(total) * facts_ref[row_count - 1 : row_count, DEV_IN : DEV_IN + 1]
    pack_ref[head, HEAD_V:, :] = jnp.broadcast_to(
        through, (pack_ref.shape[1] - HEAD_V, HEAD_K)
    ).astype(bf16)


def inner_kernel(heads, normed_ref, w_ref, kvl_ref, decay_ref, facts_ref, segrow_ref, qg_ref, inner_ref, enter_ref):
    row_count = normed_ref.shape[0]
    key_cols = heads * HEAD_K
    rows, cols, same = pair_places()
    ordered = same & (rows >= cols)
    cum_ref = decay_parts(decay_ref)[0]
    split = kvl_ref.shape[1] - LANES
    kv_ref = kvl_ref.at[:, :split]
    qg_ref[...] = mm(normed_ref[...], w_ref[:, split : 2 * split], NN)
    for head in range(heads):
        at, vat = key_at(head), value_at(head, key_cols)
        for base in range(0, row_count, PAIR):
            here = slice(base, base + PAIR)
            cum = cum_ref[here, at]
            query = qg_ref[here, at].astype(bf16).astype(f32) * HEAD_K ** (-0.5)
            query_decayed = query * jnp.exp(cum)
            key_decayed = kv_ref[here, at].astype(f32) * jnp.exp(-cum)
            visible = ordered & (facts_ref[here, SEG : SEG + 1] == segrow_ref[:, here])
            scores = jnp.where(visible, mm(query_decayed, key_decayed, NT), 0.0)
            enter_ref[here, at] = (
                query_decayed * facts_ref[here, ENTER : ENTER + 1]
            ).astype(bf16)
            inner_ref[here, value_at(head)] = mm(scores, kv_ref[here, vat], NN)


def forward_kernel(heads, hops, *refs):
    pack_refs = refs[:hops]
    qg_ref, inner_ref, enter_ref, decay_ref, facts_ref, local_ref, gain_ref, att_ref, mixed_ref, state_ref = refs[hops:]
    row_count = qg_ref.shape[0]
    spans = row_count // SPAN
    cum_ref = decay_parts(decay_ref)[0]
    gain = gain_ref[...]
    for head in range(heads):
        at, out_at = key_at(head), value_at(head)
        gate_at = value_at(head, heads * HEAD_K)
        incoming = chained(pack_refs, head)
        product = jnp.ones((1, HEAD_K), f32)
        for span in range(spans):
            here = slice(span * SPAN, (span + 1) * SPAN)
            first = slice(span * SPAN, span * SPAN + 1)
            state = (local_ref[head, span] + product * incoming).astype(bf16)
            state_ref[head, span] = state
            ending = cum_ref[span * SPAN + SPAN - 1 : span * SPAN + SPAN, at]
            product = product * (jnp.exp(ending) * facts_ref[first, KEPT : KEPT + 1])
            mixed = inner_ref[here, out_at] + mm(enter_ref[here, at], state, NT)
            mixed_ref[here, out_at] = mixed
            scale = lax.rsqrt(jnp.mean(mixed * mixed, axis=1, keepdims=True) + epsilon)
            gate = qg_ref[here, gate_at]
            att_ref[here, out_at] = (
                mixed * scale * gain * (gate * jax.nn.sigmoid(gate))
            ).astype(bf16)
        state_ref[head, spans] = (local_ref[head, spans] + product * incoming).astype(bf16)


def residual_kernel(count, *refs):
    sum_refs = refs[:count]
    hidden_ref, cot_ref, gains_ref, w_ref = refs[count : count + 4]
    grad_ref, rounded_ref, gain_ref = refs[count + 4 : count + 7]
    piece_refs = refs[count + 7 :]
    total = sum_refs[0][...].astype(f32)
    for ref in sum_refs[1:]:
        total = total + ref[...].astype(f32)
    hidden = hidden_ref[...]
    scale = lax.rsqrt(jnp.mean(hidden * hidden, axis=1, keepdims=True) + epsilon)
    gain_ref[...] = jnp.sum(total * hidden * scale, axis=0, keepdims=True)
    weighted = total * gains_ref[1:2, :]
    grad = (
        cot_ref[...].astype(f32)
        + scale * weighted
        - hidden * scale**3 * jnp.mean(weighted * hidden, axis=1, keepdims=True)
    )
    grad_ref[...] = grad
    rounded = grad.astype(bf16)
    rounded_ref[...] = rounded
    for piece in range(count):
        piece_refs[piece][...] = mm(rounded, w_ref[piece], NT).astype(bf16)


def gate_kernel(heads, count, own_rows, places_ref, *refs):
    agrad_refs = refs[:count]
    qg_ref, mixed_ref, decay_ref, facts_ref, gain_ref, mgrad_ref, gback_ref, hgain_ref, pack_ref = refs[count:]
    row_count = qg_ref.shape[0]
    run_ref = decay_parts(decay_ref)[1]
    gain = gain_ref[...]
    total = jnp.zeros((1, HEAD_V), f32)
    for head in range(heads):
        at, out_at = key_at(head), value_at(head)
        gate_at = value_at(head, heads * HEAD_K)
        state = jnp.zeros((HEAD_V, HEAD_K), f32)
        for piece in range(count):
            for base in range(0, own_rows, PAIR):
                here = pl.ds(
                    pl.multiple_of(places_ref[piece] * own_rows + base, PAIR), PAIR
                )
                mixed = mixed_ref[here, out_at]
                scale = lax.rsqrt(jnp.mean(mixed * mixed, axis=1, keepdims=True) + epsilon)
                unit = mixed * scale
                gate = qg_ref[here, gate_at]
                sig = jax.nn.sigmoid(gate)
                agrad = agrad_refs[piece][base : base + PAIR, out_at].astype(f32)
                gback_ref[here, out_at] = (
                    agrad * (unit * gain) * sig * (1.0 + gate * (1.0 - sig))
                ).astype(bf16)
                ugg = agrad * (gate * sig)
                total = total + jnp.sum(ugg * unit, axis=0, keepdims=True)
                ug = ugg * gain
                mgrad = (
                    scale * (ug - unit * jnp.mean(ug * unit, axis=1, keepdims=True))
                ).astype(bf16)
                mgrad_ref[here, out_at] = mgrad
                query = qg_ref[here, at].astype(bf16).astype(f32) * HEAD_K ** (-0.5)
                lifted = (
                    query * jnp.exp(run_ref[here, at]) * facts_ref[here, DEV_IN : DEV_IN + 1]
                )
                state = state + mm(mgrad, lifted, TN)
        put_pack(pack_ref, head, state, run_ref[row_count - 1 : row_count, at], facts_ref)
    hgain_ref[...] = total


def backward_kernel(heads, hops, *refs):
    pack_refs = refs[:hops]
    kvl_ref, qg_ref, decay_ref, facts_ref, segrow_ref, state_ref, mgrad_ref, gback_ref, up_ref = refs[hops : hops + 9]
    back_ref, bias_ref, rup_ref, after_ref, rank_ref = refs[hops + 9 :]
    query_from = kvl_ref.shape[1] - LANES
    kv_ref, low_ref = kvl_ref.at[:, :query_from], kvl_ref.at[:, query_from:]
    cum_ref, _, fpre_ref = decay_parts(decay_ref)
    rank_from = 2 * query_from
    row_count = kv_ref.shape[0]
    spans = row_count // SPAN
    key_cols = heads * HEAD_K
    rows, cols, same = pair_places()
    ordered = same & (rows >= cols)
    upper = jnp.where(same & (cols >= rows), 1.0, 0.0)
    for head in range(heads):
        at, vat, out_at = key_at(head), value_at(head, key_cols), value_at(head)
        after = chained(pack_refs, head)
        for span in reversed(range(spans)):
            here = slice(span * SPAN, (span + 1) * SPAN)
            first = slice(span * SPAN, span * SPAN + 1)
            cum = cum_ref[here, at]
            after_ref[span] = after.astype(bf16)
            query = qg_ref[here, at].astype(bf16).astype(f32) * HEAD_K ** (-0.5)
            entering = query * jnp.exp(cum) * facts_ref[here, ENTER : ENTER + 1]
            kept = jnp.exp(cum[SPAN - 1 : SPAN, :]) * facts_ref[first, KEPT : KEPT + 1]
            after = kept * after + mm(mgrad_ref[here, out_at], entering, TN)
        bias = jnp.zeros((1, HEAD_K), f32)
        rup = jnp.zeros((LANES, HEAD_K), f32)
        for base in range(0, row_count, PAIR):
            here = slice(base, base + PAIR)
            cum = cum_ref[here, at]
            query = qg_ref[here, at].astype(bf16).astype(f32) * HEAD_K ** (-0.5)
            key = kv_ref[here, at].astype(f32)
            value = kv_ref[here, vat]
            mgrad = mgrad_ref[here, out_at]
            grow = jnp.exp(cum)
            shrink = jnp.exp(-cum)
            query_decayed = (query * grow).astype(bf16)
            key_decayed = (key * shrink).astype(bf16)
            segment = facts_ref[here, SEG : SEG + 1]
            visible = ordered & (segment == segrow_ref[:, here])
            scores = jnp.where(visible, mm(query_decayed, key_decayed, NT), 0.0).astype(bf16)
            dscore = jnp.where(visible, mm(mgrad, value, NT), 0.0).astype(bf16)
            dquery_in = mm(dscore, key_decayed, NN)
            dkey_in = mm(dscore, query_decayed, TN)
            dvalue_in = mm(scores, mgrad, TN)
            terms, carries = [], []
            for half in range(PAIR // SPAN):
                mine = slice(half * SPAN, (half + 1) * SPAN)
                span = base // SPAN + half
                place = slice(span * SPAN, (span + 1) * SPAN)
                state = state_ref[head, span]
                behind = after_ref[span]
                ending = cum[(half + 1) * SPAN - 1 : (half + 1) * SPAN, :]
                tail = jnp.exp(ending - cum[mine, :]) * facts_ref[place, TAIL : TAIL + 1]
                lifted = grow[mine, :] * facts_ref[place, ENTER : ENTER + 1]
                dquery = grow[mine, :] * dquery_in[mine, :] + lifted * mm(
                    mgrad[mine, :], state, NN
                )
                dkey = shrink[mine, :] * dkey_in[mine, :] + tail * mm(
                    value[mine, :], behind, NN
                )
                dvalue = dvalue_in[mine, :] + mm(key[mine, :] * tail, behind, NT)
                back_ref[
                    place, query_from + head * HEAD_K : query_from + (head + 1) * HEAD_K
                ] = (dquery * HEAD_K ** (-0.5)).astype(bf16)
                back_ref[place, at] = dkey.astype(bf16)
                back_ref[place, vat] = dvalue.astype(bf16)
                terms.append(query[mine, :] * dquery - key[mine, :] * dkey)
                carry = jnp.sum(
                    state_ref[head, span + 1].astype(f32) * behind.astype(f32),
                    axis=0,
                    keepdims=True,
                )
                carries.append(facts_ref[place, TAIL : TAIL + 1] * carry)
            later = jnp.where(segment == segrow_ref[:, here], upper, 0.0).astype(bf16)
            decay_grad = split_mm(later, jnp.concatenate(terms, axis=0)) + jnp.concatenate(
                carries, axis=0
            )
            decay_grad = jnp.where(facts_ref[here, OPEN : OPEN + 1] > 0.0, 0.0, decay_grad)
            fgrad = decay_grad * jax.nn.sigmoid(-fpre_ref[here, at]) * (1.0 / logit_scale)
            bias = bias + jnp.sum(fgrad, axis=0, keepdims=True)
            fback = fgrad.astype(bf16)
            rup = rup + mm(low_ref[here, :], fback, TN)
            rank = mm(fback, up_ref[:, at], NT)
            if head > 0:
                rank = rank + rank_ref[here, :]
            rank_ref[here, :] = rank
        bias_ref[:, at] = bias
        rup_ref[:, at] = rup
    back_ref[:, rank_from:] = rank_ref[...].astype(bf16)
    back_ref[:, query_from + key_cols : rank_from] = gback_ref[...]


def call(kernel, outs, scratch=(), scalars=0, anywhere=0):
    def run(*args):
        specs = {}
        if scalars:
            specs["in_specs"] = [pl.BlockSpec(memory_space=pltpu.SMEM)] * scalars
            specs["in_specs"] += [pl.BlockSpec(memory_space=pltpu.HBM)] * anywhere
            specs["in_specs"] += [pl.BlockSpec()] * (len(args) - scalars - anywhere)
        return pl.pallas_call(
            kernel,
            out_shape=outs,
            scratch_shapes=list(scratch),
            compiler_params=pltpu.CompilerParams(vmem_limit_bytes=48 << 20),
            **specs,
        )(*args)

    return run


def shape_of(*dims, dtype=f32):
    return jax.ShapeDtypeStruct(dims, dtype)


def row_facts(length_row, row_count):
    seq_ends = jnp.cumsum(length_row)
    seq_starts = seq_ends - length_row
    ctx_index = lax.axis_index("ctx")
    first = ctx_index * row_count
    positions = first + jnp.arange(row_count, dtype=jnp.int32)

    def label(places):
        return jnp.sum(
            (places[:, None] >= seq_ends[None, :]).astype(jnp.int32), axis=1
        ).astype(jnp.int32)

    segment = label(positions)
    spans = row_count // SPAN
    span_first = first + jnp.arange(spans, dtype=jnp.int32) * SPAN
    before = jnp.where(span_first > 0, label(span_first - 1), -1)
    last = label(span_first + SPAN - 1)
    opening = jnp.any(positions[:, None] == seq_starts[None, :], axis=1)

    def wide(values):
        return jnp.repeat(values, SPAN)

    columns = (
        segment,
        segment == wide(before),
        segment == wide(last),
        wide(last == before),
        opening,
        segment == before[0],
        segment == last[-1],
        jnp.zeros_like(segment),
    )
    facts = jnp.stack([column.astype(f32) for column in columns], axis=1)
    return facts, segment.astype(f32)[None, :]


def rms_scale(field_in):
    return lax.rsqrt(jnp.mean(field_in * field_in, axis=-1, keepdims=True) + epsilon)


def dot(left, right, dims):
    return lax.dot_general(left, right, dims, preferred_element_type=f32)


def local(
    tokens,
    cotangent,
    lengths,
    attn_gain,
    query_proj,
    key_proj,
    value_proj,
    gate_proj,
    rank_down,
    rank_up,
    rank_bias,
    head_gain,
    output_proj,
    ffn_gain,
    ffn_gate,
    ffn_up,
    ffn_down,
):
    row_count, width = tokens.shape
    tp_count, tp_index = lax.axis_size("tp"), lax.axis_index("tp")
    own_rows = row_count // tp_count
    heads = query_proj.shape[1] // HEAD_K
    key_cols, value_cols = heads * HEAD_K, heads * HEAD_V
    both_cols = key_cols + value_cols
    shard, rank = rank_down.shape
    hops = lax.axis_size("ctx") - 1
    tp_places = numbers(around("tp"))
    row_places = places_two("fsdp", "ctx")
    count = row_places.shape[0]

    extra = -(-rank // 16) * 16
    lanes = both_cols

    def padded(values, rows, cols):
        return jnp.pad(values, ((0, rows - values.shape[0]), (0, cols - values.shape[1])))

    first = jnp.concatenate(
        [
            jnp.concatenate([key_proj, value_proj, query_proj, gate_proj], axis=1),
            jnp.concatenate(
                [
                    padded(rank_down.T, extra, lanes),
                    padded(jnp.stack([attn_gain, ffn_gain]), extra, lanes),
                ],
                axis=1,
            ),
        ],
        axis=0,
    )
    first_pieces = pass_on(pieces_of(first, "ctx"), "fsdp")
    out_shard = jnp.stack(pieces_of(output_proj, "tp"), axis=0)
    down_w = assemble(pass_on(pieces_of(ffn_down, "ctx"), "fsdp"), row_places, 1, bf16)

    facts, segrow = row_facts(lengths[0], row_count)
    up_pad = jnp.concatenate(
        [rank_up, jnp.zeros((LANES - rank, rank_up.shape[1]), bf16)], axis=0
    )
    bias_row = rank_bias.astype(f32)[None, :]
    gain_row = head_gain.astype(f32)[None, :]

    spans = row_count // SPAN
    pack_rows = HEAD_V + 16
    w, gains, normed, kvl, decays, local_states, packed = call(
        functools.partial(start_kernel, heads, count, shard, rank),
        (
            shape_of(width, 2 * both_cols + LANES, dtype=bf16),
            shape_of(8, width),
            shape_of(row_count, width, dtype=bf16),
            shape_of(row_count, both_cols + LANES, dtype=bf16),
            shape_of(row_count, 3 * key_cols),
            shape_of(heads, spans + 1, HEAD_V, HEAD_K),
            shape_of(heads, pack_rows, HEAD_K, dtype=bf16),
        ),
        (
            pltpu.VMEM((count * extra, 2 * both_cols), bf16),
            pltpu.VMEM((LANES, width), bf16),
            pltpu.SemaphoreType.DMA((2, count)),
        ),
        scalars=1,
        anywhere=count,
    )(row_places, *[outside(piece) for piece in first_pieces], tokens, up_pad, bias_row, facts)
    packs = shifted(packed, "ctx", False)
    query_gate, inner, entering = call(
        functools.partial(inner_kernel, heads),
        (
            shape_of(row_count, both_cols),
            shape_of(row_count, value_cols),
            shape_of(row_count, key_cols, dtype=bf16),
        ),
    )(normed, w, kvl, decays, facts, segrow)
    out_near = pieces_of(out_shard, "ctx")
    out_w = assemble(pass_on(out_near, "fsdp"), row_places, 2, bf16)
    attended, mixed, states = call(
        functools.partial(forward_kernel, heads, hops),
        (
            shape_of(row_count, value_cols, dtype=bf16),
            shape_of(row_count, value_cols),
            shape_of(heads, spans + 1, HEAD_V, HEAD_K, dtype=bf16),
        ),
    )(*packs, query_gate, inner, entering, decays, facts, local_states, gain_row)
    att_pieces = pieces_of(attended, "tp")
    ffn_w = assemble(
        pass_on(pieces_of(jnp.stack([ffn_gate.T, ffn_up.T], axis=0), "ctx"), "fsdp"),
        row_places,
        2,
        bf16,
    )
    inputs = tokens.astype(f32)
    hidden_full = inputs
    for hop in range(tp_count):
        hidden_full = hidden_full + dot(att_pieces[hop], out_w[hop], NN)
    gain_two = gains[1:2]

    scale_two_full = rms_scale(hidden_full)
    normed_two = (hidden_full * scale_two_full * gain_two).astype(bf16)
    gate_val = dot(normed_two, ffn_w[0], NT)
    up_val = dot(normed_two, ffn_w[1], NT)
    gate_act = jax.nn.sigmoid(gate_val)
    hidden = (gate_val * gate_act * up_val).astype(bf16)
    hidden_grad = dot(cotangent, down_w, NT)
    gate_back = (hidden_grad * up_val * gate_act * (1.0 + gate_val * (1.0 - gate_act))).astype(
        bf16
    )
    up_back = (hidden_grad * gate_val * gate_act).astype(bf16)
    two_part = (dot(gate_back, ffn_w[0], NN) + dot(up_back, ffn_w[1], NN)).astype(bf16)
    two_pieces = split(two_part, tp_places)
    two_arrived = [two_pieces[0]] + [swap(two_pieces[hop], "tp", hop) for hop in range(1, tp_count)]
    normed_two, gate_back, up_back, hidden, *_ = lax.optimization_barrier(
        (normed_two, gate_back, up_back, hidden, *two_pieces)
    )
    ffn_grads = jnp.stack(
        [
            dot(gate_back, normed_two, TN).astype(bf16),
            dot(up_back, normed_two, TN).astype(bf16),
            dot(hidden, cotangent, TN).astype(bf16),
        ],
        axis=0,
    )
    ffn_chip = collect(ffn_grads, "fsdp", 2, bf16)
    ffn_share = collect(ffn_chip, "ctx", 2, f32)
    ffn_part = dot(hidden, down_w, NN).astype(bf16)
    block_sum = reduced(ffn_part, tp_places, "tp")

    hidden_in = pick(hidden_full, tp_index, own_rows, 0)
    cotangent_own = pick(cotangent, tp_index, own_rows, 0)
    hidden_in_grad, residual_back, ffn_gain_part, *grad_pieces = call(
        functools.partial(residual_kernel, tp_count),
        (
            shape_of(own_rows, width),
            shape_of(own_rows, width, dtype=bf16),
            shape_of(1, width),
        )
        + tuple(shape_of(own_rows, value_cols, dtype=bf16) for _ in range(tp_count)),
    )(*two_arrived, hidden_in, cotangent_own, gains, out_w)
    residual_later, hidden_block, *_ = lax.optimization_barrier(
        (residual_back, hidden_in, *grad_pieces)
    )
    grad_pieces = [grad_pieces[0]] + [
        swap(grad_pieces[hop], "tp", hop) for hop in range(1, tp_count)
    ]
    mixed_grad, gate_pre_back, head_gain_part, grad_packed = call(
        functools.partial(gate_kernel, heads, tp_count, own_rows),
        (
            shape_of(row_count, value_cols, dtype=bf16),
            shape_of(row_count, value_cols, dtype=bf16),
            shape_of(1, HEAD_V),
            shape_of(heads, pack_rows, HEAD_K, dtype=bf16),
        ),
        scalars=1,
    )(tp_places, *grad_pieces, query_gate, mixed, decays, facts, gain_row)
    grad_packs = shifted(grad_packed, "ctx", True)
    back, bias_part, rank_up_part = call(
        functools.partial(backward_kernel, heads, hops),
        (
            shape_of(row_count, 2 * both_cols + LANES, dtype=bf16),
            shape_of(1, key_cols),
            shape_of(LANES, key_cols),
        ),
        (
            pltpu.VMEM((spans, HEAD_V, HEAD_K), bf16),
            pltpu.VMEM((row_count, LANES), f32),
        ),
    )(
        *grad_packs,
        kvl,
        query_gate,
        decays,
        facts,
        segrow,
        states,
        mixed_grad,
        gate_pre_back,
        up_pad,
    )
    normed_pieces = split(dot(back, w, NT).astype(bf16), tp_places)
    normed_grad = summed(normed_pieces, "tp")
    back, *_ = lax.optimization_barrier((back, *normed_pieces))

    block_own = (hidden_block + block_sum).astype(bf16)
    block_pieces = gathered(block_own, "tp")
    block_out = assemble(block_pieces, tp_places, 0, bf16, True)

    output_grads = [
        dot(pick(piece, tp_index, own_rows, 0), residual_later, TN).astype(bf16)
        for piece in att_pieces
    ]
    output_grads = jnp.stack(output_grads, axis=0)
    output_chip = collect(output_grads, "fsdp", 2, bf16)
    output_share = collect(output_chip, "ctx", 2, f32)
    attn_grads = dot(normed, back, TN).astype(bf16)
    attn_chip = collect(attn_grads, "fsdp", 0, bf16)
    attn_share = collect(attn_chip, "ctx", 0, f32)

    inputs_own = pick(tokens, tp_index, own_rows, 0).astype(f32)
    scale_own = rms_scale(inputs_own)
    attn_gain_part = jnp.sum(normed_grad * inputs_own * scale_own, axis=0)
    weighted_one = normed_grad * mark(gains)[0:1]
    tokens_own = (
        hidden_in_grad
        + scale_own * weighted_one
        - inputs_own
        * scale_own**3
        * jnp.mean(weighted_one * inputs_own, axis=-1, keepdims=True)
    ).astype(bf16)
    tokens_grad = assemble(pieces_of(tokens_own, "tp"), tp_places, 0, f32, True)

    over_all = jnp.concatenate([attn_gain_part, ffn_gain_part[0], head_gain_part[0]])
    over_rows = jnp.concatenate([rank_up_part[:rank].reshape(-1), bias_part.reshape(-1)])
    small = jnp.concatenate([over_all, over_rows]).reshape(-1, LANES)
    top = over_all.shape[0] // LANES
    small = whole_sum(whole_sum(small, "fsdp"), "ctx")
    flat = small[top:].reshape(-1)

    both_sums = jnp.concatenate(
        [
            jnp.pad(
                attn_share[:, 2 * both_cols : 2 * both_cols + rank].T,
                ((0, 0), (0, -shard % LANES)),
            ),
            small[:top],
            jnp.zeros((-(top + rank) % 16, LANES), f32),
        ],
        axis=0,
    ).astype(bf16)
    lasts = [
        jnp.concatenate(
            [
                output_share[hop].astype(bf16).reshape(-1, LANES)
                if shard % LANES == 0
                else jnp.pad(output_share[hop], ((0, 0), (0, LANES - shard))).astype(bf16),
                both_sums,
            ],
            axis=0,
        )
        for hop in range(tp_count)
    ]
    last = summed(lasts, "tp")
    output_grad = last[:value_cols, :shard]
    rank_down_grad = last[value_cols : value_cols + rank, :shard].T
    sums = last[value_cols + rank : value_cols + rank + top].reshape(-1)
    place = lax.axis_index("fsdp") * lax.axis_size("ctx") + lax.axis_index("ctx")
    return (
        block_out,
        tokens_grad,
        pick(sums[:width], place, shard, 0),
        attn_share[:, both_cols : both_cols + key_cols],
        attn_share[:, :key_cols],
        attn_share[:, key_cols:both_cols],
        attn_share[:, both_cols + key_cols : 2 * both_cols],
        rank_down_grad,
        flat[: rank * key_cols].reshape(rank, key_cols),
        flat[rank * key_cols :],
        sums[2 * width :],
        output_grad,
        pick(sums[width : 2 * width], place, shard, 0),
        ffn_share[0].T,
        ffn_share[1].T,
        ffn_share[2],
    )


def solution(mesh):
    rows = P(("fsdp", "ctx"), None)
    vector = P(("fsdp", "ctx"))
    both = P(("fsdp", "ctx"), "tp")
    turned = P("tp", ("fsdp", "ctx"))
    return jax.shard_map(
        local,
        mesh=mesh,
        in_specs=(
            rows,
            rows,
            P("fsdp", None),
            vector,
            both,
            both,
            both,
            both,
            rows,
            P(None, "tp"),
            P("tp"),
            P(),
            turned,
            vector,
            both,
            both,
            turned,
        ),
        out_specs=(
            rows,
            rows,
            vector,
            both,
            both,
            both,
            both,
            rows,
            P(None, "tp"),
            P("tp"),
            P(),
            turned,
            vector,
            both,
            both,
            turned,
        ),
        check_vma=False,
    )
```
